32 devices in a mesh: dp: 8 (over z, x), seq: 4 (over y, core).
Axes of the slice: x: 2, y: 2, z: 4, core: 2. Of those that a mesh axis runs over, the one named last changes fastest.
Arguments:
- tokens: bfloat16 [24, 512, 768], P('dp', 'seq'), may hold values from -6 to 6
- segment_ids: int32 [24, 512], P('dp'), may hold values from 0 to 7, never falling along the last dimension, each value on 1 to 128 neighbouring positions
- padding: int32 [24, 512], P('dp'), may hold values 0 or 1
- clusters: int32 [24, 12, 512], P('dp'), may hold values from 0 to 511, as said below
- w_query: bfloat16 [768, 768], replicated, may hold values from -0.4375 to 0.4375
- w_key: bfloat16 [768, 768], replicated, may hold values from -0.21875 to 0.21875
- w_value: bfloat16 [768, 768], replicated, may hold values from -0.21875 to 0.21875
- w_output: bfloat16 [768, 768], replicated, may hold values from -0.875 to 0.875
- b_query: bfloat16 [768], replicated, may hold values from -4 to 4
- b_value: bfloat16 [768], replicated, may hold values from -4 to 4
- b_output: bfloat16 [768], replicated, may hold values from -4 to 4
- gain_attn: bfloat16 [768], replicated, may hold values from 0.5 to 1.5
- shift_attn: bfloat16 [768], replicated, may hold values from -4 to 4
- w_inner: bfloat16 [768, 3072], P(None, 'seq'), may hold values from -0.21875 to 0.21875
- b_inner: bfloat16 [3072], P('seq'), may hold values from -4 to 4
- w_outer: bfloat16 [3072, 768], P('seq'), may hold values from -0.15625 to 0.15625
- b_outer: bfloat16 [768], replicated, may hold values from -4 to 4
- gain_ffn: bfloat16 [768], replicated, may hold values from 0.5 to 1.5
- shift_ffn: bfloat16 [768], replicated, may hold values from -4 to 4
- cotangent: bfloat16 [24, 512, 768], P('dp', 'seq'), may hold values from -6 to 6
Outputs:
- output: bfloat16 [24, 512, 768], P('dp', 'seq')
- grad_tokens: bfloat16 [24, 512, 768], P('dp', 'seq')
- grad_w_query: float32 [768, 768], replicated
- grad_w_key: float32 [768, 768], replicated
- grad_w_value: float32 [768, 768], replicated
- grad_w_output: float32 [768, 768], replicated
- grad_b_query: float32 [768], replicated
- grad_b_value: float32 [768], replicated
- grad_b_output: float32 [768], replicated
- grad_gain_attn: float32 [768], replicated
- grad_shift_attn: float32 [768], replicated
- grad_w_inner: float32 [768, 3072], P(None, 'seq')
- grad_b_inner: float32 [3072], P('seq')
- grad_w_outer: float32 [3072, 768], P('seq')
- grad_b_outer: float32 [768], replicated
- grad_gain_ffn: float32 [768], replicated
- grad_shift_ffn: float32 [768], replicated
- cluster_log: float32 [2, 12], replicated
The draws below stay inside these ranges and needn't reach their ends.
Inputs may be any that keep to these rules, and one draw needn't show every extreme that they name: For each row and head, clusters lists every position of the row once; each cluster of 128 consecutive entries takes at most 64 positions from each run of positions k * 128 to (k + 1) * 128 - 1, and in every row some head has a cluster that takes exactly 64 from one run.
All inputs are finite; a program needn't handle non-finite values. No bound on the sum of `padding` on one device may be relied on, other than what follows from the above.
Results may differ from the reference program's by a relative error of at most 0.018.
The reference program's roundings to bfloat16 on the way count: a program that leaves them out, or rounds other values in their place, can miss the bound.
Values may be sent and summed in bfloat16 or wider, within the bound.
No kernel may reach another device: no remote copies, remote signals or barrier semaphores. Data moves between devices by JAX's collectives and lax.ppermute only.
A program may use at most 192 MiB of HBM per device.

```python
import math
import jax
import jax.numpy as jnp
import numpy as np
from jax import lax

D = 768
HEADS = 12
HEAD = 64
FF = 3072
CLUSTER = 128
LENGTH = 512
ROWS = 24


def draw_clusters(key, part):
    shard_count = LENGTH // CLUSTER
    base_count = CLUSTER // shard_count
    key_turn, key_depth, key_head, key_order = jax.random.split(key, 4)
    turn = jax.random.randint(key_turn, (ROWS, HEADS), 0, shard_count)
    depth = jax.random.randint(key_depth, (ROWS, HEADS), 1, base_count + 1)
    chosen = jax.random.randint(key_head, (ROWS,), 0, HEADS)
    depth = jnp.where(jnp.arange(HEADS)[None, :] == chosen[:, None], base_count, depth)
    places = jnp.arange(shard_count)
    offset = (places[None, :] - places[:, None] - turn[..., None, None]) % shard_count
    counts = base_count + depth[..., None, None] * ((offset == 0).astype(jnp.int32) - (offset == 1).astype(jnp.int32))
    start = jnp.cumsum(counts, axis=2) - counts
    upper = jnp.cumsum(counts, axis=3)
    scores = jax.random.randint(key_order, (ROWS, HEADS, shard_count, CLUSTER), 0, 2 ** 20) * CLUSTER + jnp.arange(CLUSTER)
    local = jnp.argsort(scores, axis=-1).astype(jnp.int32)
    slots = jnp.arange(CLUSTER)
    source = jnp.sum((slots[:, None] >= upper[..., None, :]).astype(jnp.int32), axis=-1)
    lower = jnp.take_along_axis(upper - counts, source, axis=-1)
    begin = jnp.take_along_axis(start, source, axis=-1)
    within = begin + slots - lower
    flat_index = (source * CLUSTER + within).reshape(ROWS, HEADS, LENGTH)
    picked = jnp.take_along_axis(local.reshape(ROWS, HEADS, LENGTH), flat_index, axis=-1)
    return (picked + source.reshape(ROWS, HEADS, LENGTH) * CLUSTER).astype(jnp.int32)


def set_ends(values, stream_key, least, high):
    extent = values.shape
    index_at = [jax.random.randint(jax.random.fold_in(stream_key, axis), (), 0, extent[axis]) for axis in range(len(extent))]
    values = values.at[tuple(index_at)].set(least)
    longest = extent.index(max(extent))
    index_at[longest] = (index_at[longest] + 1) % extent[longest]
    return values.at[tuple(index_at)].set(high)


def level_of(own_key, dims, shards, low, largest):
    factor_of = 1.0
    for axis_at, blocks in shards:
        heights = jax.random.uniform(jax.random.fold_in(jax.random.fold_in(own_key, 6), axis_at), (blocks,), jnp.float32, low / len(shards), largest / len(shards))
        factor_of = factor_of * jnp.repeat(jnp.exp(heights), dims[axis_at] // blocks).reshape((-1,) + (1,) * (len(dims) - 1 - axis_at))
    return factor_of


def length_profile(amount, total, bound, slope):
    weights = [(1 << 20) // math.isqrt(rank ** slope) + 1 for rank in range(2, amount + 1)]
    spare, given = total - bound - (amount - 1), [1] * (amount - 1)
    while spare > 0:
        candidates = [i for i in range(amount - 1) if given[i] < bound]
        whole, left = sum([weights[i] for i in candidates]), spare
        for i in candidates:
            more = min(bound - given[i], max(1, left * weights[i] // whole), spare)
            given[i] = given[i] + more
            spare = spare - more
    return np.array([bound] + given)


def ragged(rng, amount, total, reach, skew):
    if amount == 2:
        one = jax.random.randint(rng, (), max(1, total - reach), min(reach, total - 1) + 1)
        return jnp.stack([one, total - one])
    sizes = jnp.asarray(length_profile(amount, total, reach, skew), jnp.int32)
    pairs = (amount - 1) // 2
    donor, sink = sizes[1:1 + 2 * pairs:2], sizes[2:2 + 2 * pairs:2]
    margin = jnp.minimum(donor - 1, reach - sink)
    shifted = jax.random.randint(jax.random.fold_in(rng, 1), (pairs,), 0, 1 << 20) % (margin + 1)
    sizes = sizes.at[1:1 + 2 * pairs:2].set(donor - shifted).at[2:2 + 2 * pairs:2].set(sink + shifted)
    return sizes[jax.random.permutation(jax.random.fold_in(rng, 2), amount)]


def normal_values(stream_key, shape, deviation, most, shards=(), held_as=jnp.bfloat16):
    values = jax.random.normal(stream_key, shape, jnp.float32) * deviation
    if len(shards) > 0:
        values = level_of(stream_key, shape, shards, -0.22, 0.18) * values
    return jnp.clip(values, min=-most, max=most).astype(held_as)


def setup_inputs(seed: int = 0) -> dict:
    seeds = jax.random.split(jax.random.key(seed), 21)
    tokens = normal_values(seeds[0], (ROWS, LENGTH, D), 1.0, 6.0, ((0, 8), (1, 4)))
    segment_ids = jax.vmap(lambda own: jnp.searchsorted(jnp.cumsum(ragged(own, 8, LENGTH, CLUSTER, 1)), jnp.arange(LENGTH), side="right"))(jax.random.split(seeds[1], ROWS)).reshape((ROWS, LENGTH)).astype(jnp.int32)
    padding = set_ends((jax.random.randint(seeds[2], (ROWS, LENGTH), 0, 8) < 7).astype(jnp.int32), jax.random.fold_in(seeds[2], 1), 0, 1)
    clusters = draw_clusters(jax.random.fold_in(seeds[20], 71), 0)
    w_query = normal_values(seeds[4], (D, D), (D // 4) ** -0.5, 0.4375)
    w_key = normal_values(seeds[5], (D, D), D ** -0.5, 0.21875)
    w_value = normal_values(seeds[6], (D, D), D ** -0.5, 0.21875)
    w_output = normal_values(seeds[7], (D, D), (D // 16) ** -0.5, 0.875)
    b_query = normal_values(seeds[8], (D,), 0.3, 4.0)
    b_value = normal_values(seeds[9], (D,), 0.3, 4.0)
    b_output = normal_values(seeds[10], (D,), 0.3, 4.0)
    gain_attn = jnp.clip(1.0 + 0.1 * jax.random.normal(seeds[11], (D,), jnp.float32), 0.5, 1.5).astype(jnp.bfloat16)
    shift_attn = normal_values(seeds[12], (D,), 0.3, 4.0)
    w_inner = normal_values(seeds[13], (D, FF), D ** -0.5, 0.21875, ((1, 4),))
    b_inner = normal_values(seeds[14], (FF,), 0.3, 4.0, ((0, 4),))
    w_outer = normal_values(seeds[15], (FF, D), (FF // 2) ** -0.5, 0.15625, ((0, 4),))
    b_outer = normal_values(seeds[16], (D,), 0.3, 4.0)
    gain_ffn = jnp.clip(1.0 + 0.1 * jax.random.normal(seeds[17], (D,), jnp.float32), 0.5, 1.5).astype(jnp.bfloat16)
    shift_ffn = normal_values(seeds[18], (D,), 0.3, 4.0)
    cotangent = normal_values(seeds[19], (ROWS, LENGTH, D), 1.0, 6.0, ((0, 8), (1, 4)))
    return dict(tokens=tokens, segment_ids=segment_ids, padding=padding, clusters=clusters, w_query=w_query, w_key=w_key, w_value=w_value, w_output=w_output, b_query=b_query, b_value=b_value, b_output=b_output, gain_attn=gain_attn, shift_attn=shift_attn, w_inner=w_inner, b_inner=b_inner, w_outer=w_outer, b_outer=b_outer, gain_ffn=gain_ffn, shift_ffn=shift_ffn, cotangent=cotangent)


@jax.custom_vjp
def low(v):
    return lax.optimization_barrier(v.astype(jnp.bfloat16)).astype(jnp.float32)

@jax.custom_vjp
def low_back(v):
    return v

def low_keep(v):
    return (low(v), None)

def low_pass(kept, grad):
    return (grad,)

def back_keep(v):
    return (v, None)

def back_low(kept, grad):
    return (low(grad),)
low.defvjp(low_keep, low_pass)
low_back.defvjp(back_keep, back_low)
EPSILON = 1e-12
NEGATIVE = -1e+30
HIGH = lax.Precision.HIGHEST

def norm_rows(value, gain, shift):
    center = lax.optimization_barrier(jnp.mean(value, axis=-1, keepdims=True))
    centred = value - center
    spread = lax.optimization_barrier(jnp.mean(centred * centred, axis=-1, keepdims=True))
    return centred * lax.rsqrt(spread + EPSILON) * gain + shift

def project(left, right):
    return jnp.einsum('rtd,de->rte', left, right, precision=HIGH)

def cluster_attention(queries, keys, values, segment_ids, padding, clusters):
    group_size, length, head_count, head_width = queries.shape
    groups = length // CLUSTER

    def pick(field):
        moved = jnp.transpose(field, (0, 2, 1, 3))
        taken = jnp.take_along_axis(moved, clusters[..., None], axis=2)
        return taken.reshape(group_size, head_count, groups, CLUSTER, head_width)
    q_clus, k_clus, v_clus = (pick(queries), pick(keys), pick(values))
    full_shape = (group_size, head_count, length)
    seg_clus = jnp.take_along_axis(jnp.broadcast_to(segment_ids[:, None, :], full_shape), clusters, axis=2)
    pad_clus = jnp.take_along_axis(jnp.broadcast_to(padding[:, None, :], full_shape), clusters, axis=2)
    seg_clus = seg_clus.reshape(group_size, head_count, groups, CLUSTER)
    pad_clus = pad_clus.reshape(group_size, head_count, groups, CLUSTER)
    scores = low_back(jnp.einsum('ghcid,ghcjd->ghcij', q_clus, k_clus, precision=HIGH))
    same_doc = seg_clus[..., :, None] == seg_clus[..., None, :]
    diagonal = jnp.eye(CLUSTER, dtype=bool)
    allowed = same_doc & ((pad_clus[..., None, :] == 1) | diagonal)
    masked = jnp.where(allowed, scores, NEGATIVE)
    top = lax.optimization_barrier(jnp.max(masked, axis=-1, keepdims=True))
    lse = top + jnp.log(lax.optimization_barrier(jnp.sum(jnp.exp(masked - top), axis=-1, keepdims=True)))
    prob = jnp.exp(masked - lse)
    result = jnp.einsum('ghcij,ghcjd->ghcid', low(prob), v_clus, precision=HIGH)
    entropy = lse[..., 0] - lax.optimization_barrier(jnp.sum(prob * jnp.where(allowed, scores, 0.0), axis=-1))
    key_log = jnp.log(lax.optimization_barrier(jnp.sum(allowed.astype(jnp.float32), axis=-1)))
    real = (pad_clus == 1).astype(jnp.float32)
    stats = jnp.stack([lax.optimization_barrier(jnp.sum(entropy * real, axis=(0, 2, 3))), lax.optimization_barrier(jnp.sum(key_log * real, axis=(0, 2, 3))), lax.optimization_barrier(jnp.sum(real, axis=(0, 2, 3)))])
    result = result.reshape(group_size, head_count, length, head_width)
    inverse = jnp.argsort(clusters, axis=-1).astype(jnp.int32)
    placed = jnp.take_along_axis(result, inverse[..., None], axis=2)
    placed = jnp.transpose(placed, (0, 2, 1, 3)).reshape(group_size, length, head_count * head_width)
    return (placed, stats)

def layer(tokens, w_query, w_key, w_value, w_output, b_query, b_value, b_output, gain_attn, shift_attn, w_inner, b_inner, w_outer, b_outer, gain_ffn, shift_ffn, segment_ids, padding, clusters):
    group_size = tokens.shape[0]
    shape_four = (group_size, LENGTH, HEADS, HEAD)
    queries = low_back(low((project(tokens, w_query) + b_query) * 0.125))
    keys = low_back(low(project(tokens, w_key)))
    values = low_back(low(project(tokens, w_value) + b_value))
    context, stats = cluster_attention(queries.reshape(shape_four), keys.reshape(shape_four), values.reshape(shape_four), segment_ids, padding, clusters)
    context = low_back(low(context))
    attended = low_back(project(context, w_output)) + b_output
    middle = norm_rows(tokens + attended, gain_attn, shift_attn)
    pre = low_back(project(low(middle), w_inner) + b_inner)
    act = low(jax.nn.gelu(pre, approximate=False))
    ffn = low_back(project(act, w_outer)) + b_outer
    return (norm_rows(middle + ffn, gain_ffn, shift_ffn), stats)

def reference(tokens, segment_ids, padding, clusters, w_query, w_key, w_value, w_output, b_query, b_value, b_output, gain_attn, shift_attn, w_inner, b_inner, w_outer, b_outer, gain_ffn, shift_ffn, cotangent):
    group_size = math.gcd(ROWS, max(1, 4096 // LENGTH))
    weights = tuple((w.astype(jnp.float32) for w in (w_query, w_key, w_value, w_output, b_query, b_value, b_output, gain_attn, shift_attn, w_inner, b_inner, w_outer, b_outer, gain_ffn, shift_ffn)))

    def one_block(carry, batch):
        block_tokens, block_segs, block_pads, block_clusters, block_cot = batch

        def forward(tok_value, *params):
            return layer(tok_value, *params, block_segs, block_pads, block_clusters)
        result, pull, stats = jax.vjp(forward, block_tokens.astype(jnp.float32), *weights, has_aux=True)
        grads = pull(block_cot.astype(jnp.float32))
        summed = tuple((acc + new for acc, new in zip(carry[0], grads[1:])))
        return ((summed, carry[1] + stats), (result.astype(jnp.bfloat16), grads[0].astype(jnp.bfloat16)))

    def blocks(array):
        return array.reshape((ROWS // group_size, group_size) + array.shape[1:])
    init = (tuple((jnp.zeros_like(w) for w in weights)), jnp.zeros((3, HEADS), jnp.float32))
    (sums, stats), (outputs, grad_in) = lax.scan(one_block, init, (blocks(tokens), blocks(segment_ids), blocks(padding), blocks(clusters), blocks(cotangent)))
    output = outputs.reshape(ROWS, LENGTH, D)
    grad_tokens = grad_in.reshape(ROWS, LENGTH, D)
    cluster_log = stats[0:2] / stats[2:3]
    return (output, grad_tokens, sums[0], sums[1], sums[2], sums[3], sums[4], sums[5], sums[6], sums[7], sums[8], sums[9], sums[10], sums[11], sums[12], sums[13], sums[14], cluster_log)
```

```python
import jax
import jax.numpy as jnp
from jax import lax
from jax.experimental import pallas as pl
from jax.experimental.pallas import tpu as pltpu
from jax.sharding import PartitionSpec as P

EPSILON = 1e-12
NEGATIVE = -1e30
LANES = 128
AXES = ("dp", "seq")
F32 = jnp.float32
BF16 = jnp.bfloat16


def dot_nn(left, right):
    return lax.dot_general(left, right, (((1,), (0,)), ((), ())), preferred_element_type=F32)


def dot_nt(left, right):
    return lax.dot_general(left, right, (((1,), (1,)), ((), ())), preferred_element_type=F32)


def dot_tn(left, right):
    return lax.dot_general(left, right, (((0,), (0,)), ((), ())), preferred_element_type=F32)


def codes_kernel(where_ref, cl_ref, seg_ref, pad_ref, qrow_ref, krow_ref, qcol_ref, kcol_ref):
    head_count = cl_ref.shape[1]
    length = cl_ref.shape[2]
    spot = lax.broadcasted_iota(jnp.int32, (LANES, length), 0)
    line = lax.broadcasted_iota(jnp.int32, (8, length), 0)
    cluster = lax.broadcasted_iota(jnp.int32, (8, length), 1) // LANES
    anchors = [where_ref[0], where_ref[1], where_ref[2]]
    edge_ok = where_ref[3] == 1
    want = jnp.where(line == 0, anchors[0], jnp.where(line == 1, anchors[1], anchors[2]))
    want = jnp.where(line < 3, want, -1)
    qrow_ref[...] = jnp.full(qrow_ref.shape, -2.0, F32)
    krow_ref[...] = jnp.full(krow_ref.shape, -1.0, F32)
    segs, pads = [], []
    for block in range(3):
        start = pl.multiple_of(anchors[block] * LANES, LANES)
        segs.append(seg_ref[0, :, pl.ds(start, LANES)].astype(F32))
        pads.append(pad_ref[0, :, pl.ds(start, LANES)])
    for head in range(head_count):
        members = cl_ref[0, head : head + 1, :]
        onehot = (spot == (members % LANES)).astype(F32).astype(BF16)
        chosen = jnp.where((members // LANES) == want, cluster, 0).astype(F32).astype(BF16)
        found = dot_nt(chosen, onehot)
        for block in range(3):
            code = found[block : block + 1, :] * 8.0 + segs[block]
            query, key = code, jnp.where(pads[block] == 1, code, -1.0)
            if block == 2:
                query = jnp.where(edge_ok, query, -2.0)
                key = jnp.where(edge_ok, key, -1.0)
            at = block * 16 + head
            qrow_ref[0, at : at + 1, :] = query
            krow_ref[0, at : at + 1, :] = key
    qrow_ref[0, 48:49, :] = (pads[0] == 1).astype(F32)
    qcol_ref[0] = qrow_ref[0].T
    kcol_ref[0] = krow_ref[0].T


def cluster_codes(clusters, segment_ids, padding, where_at):
    row_count, head_count, length = clusters.shape
    table = jax.ShapeDtypeStruct((row_count, LANES, LANES), F32)
    spec = pl.BlockSpec((1, LANES, LANES), lambda r, w: (r, 0, 0))
    return pl.pallas_call(
        codes_kernel,
        out_shape=(table,) * 4,
        grid_spec=pltpu.PrefetchScalarGridSpec(
            num_scalar_prefetch=1,
            grid=(row_count,),
            in_specs=[
                pl.BlockSpec((1, head_count, length), lambda r, w: (r, 0, 0)),
                pl.BlockSpec((1, 1, length), lambda r, w: (r, 0, 0)),
                pl.BlockSpec((1, 1, length), lambda r, w: (r, 0, 0)),
            ],
            out_specs=[spec] * 4,
        ),
        name="codes",
    )(where_at, clusters, segment_ids[:, None, :], padding[:, None, :])


def halves(value):
    low = lax.broadcasted_iota(jnp.int32, value.shape, 1) < (LANES // 2)
    zero = jnp.zeros_like(value)
    return jnp.where(low, value, zero), jnp.where(low, zero, value)


def pick(even, odd):
    return jnp.where(lax.broadcasted_iota(jnp.int32, even.shape, 1) < (LANES // 2), even, odd)


def diagonal():
    return lax.broadcasted_iota(jnp.int32, (LANES, LANES), 0) == lax.broadcasted_iota(
        jnp.int32, (LANES, LANES), 1
    )


def attend_kernel(model, q_ref, k_ref, v_ref, kh_ref, vh_ref, krow_ref, qcol_ref, ctx_ref, lse_ref, stat_ref):
    eye = diagonal()
    lane = lax.broadcasted_iota(jnp.int32, (LANES, LANES), 1)
    lse_all = jnp.zeros((LANES, LANES), F32)
    entropy_all = jnp.zeros((LANES, LANES), F32)
    count_all = jnp.ones((LANES, LANES), F32)
    for pair in range(model // LANES):
        at = slice(pair * LANES, (pair + 1) * LANES)
        queries = halves(q_ref[0, :, at])
        keys = jnp.concatenate([k_ref[0, :, at], kh_ref[0, 0, :, at], kh_ref[1, 0, :, at]], axis=0)
        values = jnp.concatenate([v_ref[0, :, at], vh_ref[0, 0, :, at], vh_ref[1, 0, :, at]], axis=0)
        out = []
        for side in range(2):
            head = pair * 2 + side
            raw = dot_nt(queries[side], keys)
            code = qcol_ref[0, :, head : head + 1]
            allowed = [code == krow_ref[0, b * 16 + head : b * 16 + head + 1, :] for b in range(3)]
            allowed[0] = allowed[0] | eye
            allowed = jnp.concatenate(allowed, axis=1)
            masked = jnp.where(allowed, raw, NEGATIVE)
            top = jnp.max(masked, axis=1, keepdims=True)
            grown = jnp.exp(masked - top)
            total = jnp.sum(grown, axis=1, keepdims=True)
            prob = grown * (1.0 / total)
            lse = top + jnp.log(total)
            entropy = lse - jnp.sum(prob * masked, axis=1, keepdims=True)
            count = jnp.sum(jnp.where(allowed, 1.0, 0.0), axis=1, keepdims=True)
            out.append(dot_nn(prob.astype(BF16), values))
            lse_all = jnp.where(lane == head, lse, lse_all)
            entropy_all = jnp.where(lane == head, entropy, entropy_all)
            count_all = jnp.where(lane == head, count, count_all)
        ctx_ref[0, :, at] = pick(out[0], out[1]).astype(BF16)
    real = qcol_ref[0, :, 48:49]
    stat_ref[0] = jnp.zeros(stat_ref.shape[1:], F32)
    stat_ref[0, 0:1, :] = jnp.sum(entropy_all * real, axis=0, keepdims=True)
    stat_ref[0, 1:2, :] = jnp.sum(jnp.log(count_all) * real, axis=0, keepdims=True)
    stat_ref[0, 2:3, :] = jnp.sum(jnp.broadcast_to(real, (LANES, LANES)), axis=0, keepdims=True)
    lse_ref[0] = lse_all.T[:16, :]


def attend(q, k, v, kh, vh, krow, qcol):
    row_count, shard_len, model = q.shape
    own = pl.BlockSpec((1, shard_len, model), lambda r: (r, 0, 0))
    near = pl.BlockSpec((2, 1, shard_len, model), lambda r: (0, r, 0, 0))
    table = pl.BlockSpec((1, LANES, LANES), lambda r: (r, 0, 0))
    return pl.pallas_call(
        lambda *refs: attend_kernel(model, *refs),
        out_shape=(
            jax.ShapeDtypeStruct(q.shape, BF16),
            jax.ShapeDtypeStruct((row_count, 16, LANES), F32),
            jax.ShapeDtypeStruct((row_count, 8, LANES), F32),
        ),
        grid=(row_count,),
        in_specs=[own, own, own, near, near, table, table],
        out_specs=(
            own,
            pl.BlockSpec((1, 16, LANES), lambda r: (r, 0, 0)),
            pl.BlockSpec((1, 8, LANES), lambda r: (r, 0, 0)),
        ),
        name="attend",
    )(q, k, v, kh, vh, krow, qcol)


def pull_kernel(
    model,
    q_ref,
    k_ref,
    v_ref,
    d_ref,
    qh_ref,
    kh_ref,
    vh_ref,
    dc_ref,
    de_ref,
    row_ref,
    rowc_ref,
    rowe_ref,
    qrow_ref,
    krow_ref,
    qcol_ref,
    kcol_ref,
    out_ref,
    bias_ref,
):
    eye = diagonal()
    cols = jnp.concatenate([row_ref[0], jnp.zeros((LANES - 32, LANES), F32)], axis=0).T
    bias_ref[0] = jnp.zeros(bias_ref.shape[1:], F32)
    for pair in range(model // LANES):
        at = slice(pair * LANES, (pair + 1) * LANES)
        q_own, k_own, v_own, d_own = q_ref[0, :, at], k_ref[0, :, at], v_ref[0, :, at], d_ref[0, :, at]
        queries, grads = halves(q_own), halves(d_own)
        k_all = jnp.concatenate([k_own, kh_ref[0, 0, :, at], kh_ref[1, 0, :, at]], axis=0)
        v_all = jnp.concatenate([v_own, vh_ref[0, 0, :, at], vh_ref[1, 0, :, at]], axis=0)
        q_all = jnp.concatenate([q_own, qh_ref[0, 0, :, at], qh_ref[1, 0, :, at]], axis=0)
        d_all = jnp.concatenate([d_own, dc_ref[0, :, at], de_ref[0, :, at]], axis=0)
        keys, values = halves(k_own), halves(v_own)
        dq, dk, dv = [], [], []
        for side in range(2):
            head = pair * 2 + side
            code = qcol_ref[0, :, head : head + 1]
            allowed = [code == krow_ref[0, b * 16 + head : b * 16 + head + 1, :] for b in range(3)]
            allowed[0] = allowed[0] | eye
            raw = dot_nt(queries[side], k_all)
            lse, delta = cols[:, head : head + 1], cols[:, 16 + head : 17 + head]
            prob = jnp.exp(jnp.where(jnp.concatenate(allowed, axis=1), raw, NEGATIVE) - lse)
            d_score = (prob * (dot_nt(grads[side], v_all) - delta)).astype(BF16)
            dq.append(dot_nn(d_score, k_all))

            code = kcol_ref[0, :, head : head + 1]
            allowed = [code == qrow_ref[0, b * 16 + head : b * 16 + head + 1, :] for b in range(3)]
            allowed[0] = allowed[0] | eye
            raw = dot_nt(keys[side], q_all)
            lse = jnp.concatenate([r[0, head : head + 1, :] for r in (row_ref, rowc_ref, rowe_ref)], axis=1)
            delta = jnp.concatenate(
                [r[0, 16 + head : 17 + head, :] for r in (row_ref, rowc_ref, rowe_ref)], axis=1
            )
            prob = jnp.exp(jnp.where(jnp.concatenate(allowed, axis=1), raw, NEGATIVE) - lse)
            d_score = (prob * (dot_nt(values[side], d_all) - delta)).astype(BF16)
            dk.append(dot_nn(d_score, q_all))
            dv.append(dot_nn(prob.astype(BF16), d_all))
        for index, (both, scale) in enumerate(((dq, 0.125), (dk, 1.0), (dv, 1.0))):
            low = pick(both[0], both[1]).astype(BF16)
            wide = low.astype(F32) * scale
            spot = slice(index * model + pair * LANES, index * model + (pair + 1) * LANES)
            out_ref[0, :, spot] = wide.astype(BF16)
            bias_ref[0, 0:1, spot] = jnp.sum(wide, axis=0, keepdims=True)


def pull(q, k, v, d, qh, kh, vh, dc, de, row, rowc, rowe, qrow, krow, qcol, kcol):
    row_count, shard_len, model = q.shape
    own = pl.BlockSpec((1, shard_len, model), lambda r: (r, 0, 0))
    near = pl.BlockSpec((2, 1, shard_len, model), lambda r: (0, r, 0, 0))
    table = pl.BlockSpec((1, LANES, LANES), lambda r: (r, 0, 0))
    lines = pl.BlockSpec((1, 32, LANES), lambda r: (r, 0, 0))
    return pl.pallas_call(
        lambda *refs: pull_kernel(model, *refs),
        out_shape=(
            jax.ShapeDtypeStruct((row_count, shard_len, 3 * model), BF16),
            jax.ShapeDtypeStruct((row_count, 8, 3 * model), F32),
        ),
        grid=(row_count,),
        in_specs=[own] * 4 + [near] * 3 + [own] * 2 + [lines] * 3 + [table] * 4,
        out_specs=(
            pl.BlockSpec((1, shard_len, 3 * model), lambda r: (r, 0, 0)),
            pl.BlockSpec((1, 8, 3 * model), lambda r: (r, 0, 0)),
        ),
        name="pull",
    )(q, k, v, d, qh, kh, vh, dc, de, row, rowc, rowe, qrow, krow, qcol, kcol)


def normed(value):
    centred = value - jnp.mean(value, axis=-1, keepdims=True)
    inverse = lax.rsqrt(jnp.mean(centred * centred, axis=-1, keepdims=True) + EPSILON)
    return centred * inverse, inverse


def norm_pull(grad, gain, unit, inverse):
    scaled = grad * gain
    moved = scaled - jnp.mean(scaled, axis=-1, keepdims=True)
    moved = moved - unit * jnp.mean(scaled * unit, axis=-1, keepdims=True)
    return moved * inverse


def gelu_both(value):
    cdf = 0.5 * lax.erfc(value * (-(0.5**0.5)))
    density = jnp.exp(-0.5 * value * value) * 0.3989422804014327
    return value * cdf, cdf + value * density


class Links:
    def __init__(self, dp_size, seq_size):
        self.dp, self.seq = dp_size, seq_size
        self.dp_at, self.seq_at = lax.axis_index("dp"), lax.axis_index("seq")
        stages, stride = [(1, 2)], 2
        while stride < dp_size:
            radix = min(4, dp_size // stride)
            stages.append((stride, radix))
            stride *= radix
        self.stages = stages

    def swap(self, value, dp_bits, seq_bits):
        pairs = [
            (d * self.seq + s, (d ^ dp_bits) * self.seq + (s ^ seq_bits))
            for d in range(self.dp)
            for s in range(self.seq)
        ]
        return lax.ppermute(value, AXES, pairs)

    def edge(self, value):
        pairs = []
        for d in range(self.dp):
            for s in range(1, self.seq - 1, 2):
                pairs.append((d * self.seq + s, d * self.seq + s + 1))
                pairs.append((d * self.seq + s + 1, d * self.seq + s))
        return lax.ppermute(value, AXES, pairs)

    def dp_stage(self, stage):
        stride, radix = stage
        return [(j * stride, 0) for j in range(radix)], (self.dp_at // stride) % radix

    def plane(self):
        return [(j & 1, (j >> 1) * 2) for j in range(4)], (self.dp_at % 2) + 2 * (self.seq_at // 2)

    def spread(self, value, stage):
        partners, mine = stage
        rows = value.shape[0] // len(partners)
        total = lax.dynamic_slice_in_dim(value, mine * rows, rows, 0).astype(F32)
        for index in range(1, len(partners)):
            sent = lax.dynamic_slice_in_dim(value, (mine ^ index) * rows, rows, 0)
            total = total + self.swap(sent, *partners[index]).astype(F32)
        return total.astype(BF16)

    def collect(self, value, stage, dtype=BF16):
        partners, mine = stage
        rows = value.shape[0]
        whole = jnp.zeros((rows * len(partners),) + value.shape[1:], dtype)
        for index in range(len(partners)):
            piece = self.swap(value, *partners[index]) if index else value
            whole = lax.dynamic_update_slice_in_dim(whole, piece.astype(dtype), (mine ^ index) * rows, 0)
        return whole

    def core_spread(self, value):
        mine = self.seq_at % 2
        cols = value.shape[1] // 2
        keep = lax.dynamic_slice_in_dim(value, mine * cols, cols, 1)
        sent = lax.dynamic_slice_in_dim(value, (1 - mine) * cols, cols, 1)
        return (keep.astype(F32) + self.swap(sent, 0, 1).astype(F32)).astype(BF16)

    def core_collect(self, value):
        mine = self.seq_at % 2
        other = self.swap(value, 0, 1)
        first = jnp.where(mine == 0, value, other)
        second = jnp.where(mine == 0, other, value)
        return jnp.concatenate([first, second], axis=1).astype(F32)

    def total(self, value):
        for bits in (1, 2):
            value = value + self.swap(value, 0, bits)
        stride = 1
        while stride < self.dp:
            value = value + self.swap(value, stride, 0)
            stride *= 2
        return value

    def everywhere(self, value):
        value = self.core_spread(value)
        stages = [self.plane()] + [self.dp_stage(s) for s in self.stages[1:]]
        for stage in stages:
            value = self.spread(value, stage)
        for stage in reversed(stages):
            value = self.collect(value, stage)
        return self.core_collect(value)

    def over_dp(self, value):
        stages = [self.dp_stage(s) for s in self.stages]
        for stage in stages:
            value = self.spread(value, stage)
        for stage in reversed(stages[1:]):
            value = self.collect(value, stage)
        return self.collect(value, stages[0], F32)


def body(
    tokens,
    segment_ids,
    padding,
    clusters,
    w_query,
    w_key,
    w_value,
    w_output,
    b_query,
    b_value,
    b_output,
    gain_attn,
    shift_attn,
    w_inner,
    b_inner,
    w_outer,
    b_outer,
    gain_ffn,
    shift_ffn,
    cotangent,
):
    links = Links(lax.axis_size("dp"), lax.axis_size("seq"))
    seq_at, seq_count = links.seq_at, links.seq
    row_count, shard_len, model = tokens.shape
    head_count = clusters.shape[1]
    amount = row_count * shard_len
    near = jnp.stack([links.swap(tokens, 0, 1), links.edge(tokens)])
    partner = seq_at ^ 1
    edge_raw = jnp.where(seq_at % 2 == 1, seq_at + 1, seq_at - 1)
    edge_ok = (edge_raw >= 0) & (edge_raw < seq_count)
    edge_at = jnp.clip(edge_raw, 0, seq_count - 1)
    where_at = jnp.stack([seq_at, partner, edge_at, edge_ok.astype(seq_at.dtype)]).astype(jnp.int32)
    qrow, krow, qcol, kcol = cluster_codes(clusters, segment_ids, padding, where_at)

    inner, outer, inner_bias = [w_inner], [w_outer], [b_inner[None, :]]
    inner.append(links.swap(inner[0], 0, 2))
    outer.append(links.swap(outer[0], 0, 2))
    inner_bias.append(links.swap(inner_bias[0], 0, 2))
    for index in range(2):
        inner.append(links.swap(inner[index], 0, 1))
        outer.append(links.swap(outer[index], 0, 1))
        inner_bias.append(links.swap(inner_bias[index], 0, 1))

    def make_query(array):
        return ((dot_nn(array, w_query) + b_query.astype(F32)) * 0.125).astype(BF16)

    def make_key(array):
        return dot_nn(array, w_key).astype(BF16)

    def make_value(array):
        return (dot_nn(array, w_value) + b_value.astype(F32)).astype(BF16)

    flat = tokens.reshape(amount, model)
    flat_near = near.reshape(2 * amount, model)
    own_shape = (row_count, shard_len, model)
    near_shape = (2,) + own_shape
    q = make_query(flat).reshape(own_shape)
    k = make_key(flat).reshape(own_shape)
    v = make_value(flat).reshape(own_shape)
    kh = make_key(flat_near).reshape(near_shape)
    vh = make_value(flat_near).reshape(near_shape)
    context, lse, stats = attend(q, k, v, kh, vh, krow, qcol)
    qh = make_query(flat_near).reshape(near_shape)
    context = context.reshape(amount, model)

    x = flat.astype(F32)
    residual_one = x + dot_nn(context, w_output) + b_output.astype(F32)
    unit_one, inverse_one = normed(residual_one)
    gain_one = gain_attn.astype(F32)
    mid = unit_one * gain_one + shift_attn.astype(F32)
    mid_low = mid.astype(BF16)

    acts, slopes = [], []
    residual_two = mid + b_outer.astype(F32)
    for index in range(4):
        pre = dot_nn(mid_low, inner[index]) + inner_bias[index].astype(F32)
        act, slope = gelu_both(pre)
        acts.append(act.astype(BF16))
        slopes.append(slope)
        residual_two = residual_two + dot_nn(acts[index], outer[index])
    unit_two, inverse_two = normed(residual_two)
    gain_two = gain_ffn.astype(F32)
    output = (unit_two * gain_two + shift_ffn.astype(F32)).astype(BF16)
    grad = cotangent.reshape(amount, model).astype(F32)
    d_two = norm_pull(grad, gain_two, unit_two, inverse_two)
    d_two_low = d_two.astype(BF16)

    d_mid = d_two
    grads_inner, grads_outer, grads_bias = [None] * 4, [None] * 4, [None] * 4
    for index in (3, 1, 2, 0):
        d_pre = (slopes[index] * dot_nt(d_two_low, outer[index])).astype(BF16)
        grads_outer[index] = dot_tn(acts[index], d_two_low)
        grads_inner[index] = dot_tn(mid_low, d_pre)
        grads_bias[index] = jnp.sum(d_pre.astype(F32), axis=0)
        d_mid = d_mid + dot_nt(d_pre, inner[index])

    def own_sum(parts):
        far = parts[1] + links.swap(parts[3].astype(BF16), 0, 1).astype(F32)
        here = parts[0] + links.swap(parts[2].astype(BF16), 0, 1).astype(F32)
        return (here + links.swap(far.astype(BF16), 0, 2).astype(F32)).astype(BF16)

    grad_outer = links.over_dp(own_sum(grads_outer))
    grad_inner = links.over_dp(own_sum(grads_inner))

    d_one = norm_pull(d_mid, gain_one, unit_one, inverse_one)
    d_one_low = d_one.astype(BF16)
    d_context = dot_nt(d_one_low, w_output).astype(BF16)
    grad_w_output = links.everywhere(dot_tn(context, d_one_low).astype(BF16))
    head_of = lax.broadcasted_iota(jnp.int32, (16, model), 1) // (model // head_count)
    head_sum = (head_of == lax.broadcasted_iota(jnp.int32, (16, model), 0)).astype(F32)
    delta = lax.dot_general(
        head_sum,
        d_context.astype(F32) * context.astype(F32),
        (((1,), (1,)), ((), ())),
        precision=lax.Precision.HIGHEST,
        preferred_element_type=F32,
    )
    delta = jnp.transpose(delta.reshape(16, row_count, shard_len), (1, 0, 2))
    d_context = d_context.reshape(own_shape)
    lines = jnp.concatenate([lse, delta], axis=1)
    d_qkv, d_bias = pull(
        q,
        k,
        v,
        d_context,
        qh,
        kh,
        vh,
        links.swap(d_context, 0, 1),
        links.edge(d_context),
        lines,
        links.swap(lines, 0, 1),
        links.edge(lines),
        qrow,
        krow,
        qcol,
        kcol,
    )
    d_qkv = d_qkv.reshape(amount, 3 * model)
    grad_qkv = links.everywhere(dot_tn(flat, d_qkv).astype(BF16))
    grad_tokens = (
        d_one
        + dot_nt(d_qkv[:, :model], w_query)
        + dot_nt(d_qkv[:, model : 2 * model], w_key)
        + dot_nt(d_qkv[:, 2 * model :], w_value)
    ).astype(BF16)

    def placed(bits):
        order = [bits[0], bits[2], bits[1], bits[3]]
        stacked = jnp.stack(order)
        return jnp.stack([lax.dynamic_index_in_dim(stacked, seq_at ^ a, 0, False) for a in range(4)])

    d_bias = jnp.sum(d_bias[:, 0, :], axis=0)
    stat_rows = jnp.sum(stats, axis=0)[0:3, :]
    stat_rows = jnp.pad(stat_rows, ((0, 0), (0, model - LANES)))
    small = jnp.stack(
        [
            d_bias[:model],
            d_bias[2 * model :],
            jnp.sum(d_one, axis=0),
            jnp.sum(d_mid * unit_one, axis=0),
            jnp.sum(d_mid, axis=0),
            jnp.sum(d_two, axis=0),
            jnp.sum(grad * unit_two, axis=0),
            jnp.sum(grad, axis=0),
        ]
    )
    small = links.total(jnp.concatenate([small, stat_rows, placed(grads_bias)], axis=0))
    cluster_log = small[8:10, :head_count] / small[10:11, 0:1]
    return (
        output.reshape(own_shape),
        grad_tokens.reshape(own_shape),
        grad_qkv[:, :model],
        grad_qkv[:, model : 2 * model],
        grad_qkv[:, 2 * model :],
        grad_w_output,
        small[0],
        small[1],
        small[2],
        small[3],
        small[4],
        grad_inner,
        lax.dynamic_index_in_dim(small[11:15], seq_at, 0, False),
        grad_outer,
        small[5],
        small[6],
        small[7],
        cluster_log,
    )


def solution(mesh):
    return jax.shard_map(
        body,
        mesh=mesh,
        in_specs=(
            P("dp", "seq", None),
            P("dp", None),
            P("dp", None),
            P("dp", None, None),
            P(),
            P(),
            P(),
            P(),
            P(),
            P(),
            P(),
            P(),
            P(),
            P(None, "seq"),
            P("seq"),
            P("seq", None),
            P(),
            P(),
            P(),
            P("dp", "seq", None),
        ),
        out_specs=(
            P("dp", "seq", None),
            P("dp", "seq", None),
            P(),
            P(),
            P(),
            P(),
            P(),
            P(),
            P(),
            P(),
            P(),
            P(None, "seq"),
            P("seq"),
            P("seq", None),
            P(),
            P(),
            P(),
            P(),
        ),
        check_vma=False,
    )
```

```python
import jax
import jax.numpy as jnp
from jax import lax
from jax.experimental import pallas as pl
from jax.experimental.pallas import tpu as pltpu
from jax.sharding import PartitionSpec as P


EPSILON = 1e-12
NEGATIVE = -1e30
LANES = 128
AXES = ("dp", "seq")
F32 = jnp.float32
BF16 = jnp.bfloat16


def dot_nn(left, right):
    return lax.dot_general(left, right, (((1,), (0,)), ((), ())), preferred_element_type=F32)


def dot_nt(left, right):
    return lax.dot_general(left, right, (((1,), (1,)), ((), ())), preferred_element_type=F32)


def dot_tn(left, right):
    return lax.dot_general(left, right, (((0,), (0,)), ((), ())), preferred_element_type=F32)


def codes_kernel(where_ref, cl_ref, seg_ref, pad_ref, qrow_ref, krow_ref, qcol_ref, kcol_ref):
    row = pl.program_id(0)
    head_count = cl_ref.shape[1]
    length = cl_ref.shape[2]
    spot = lax.broadcasted_iota(jnp.int32, (LANES, length), 0)
    line = lax.broadcasted_iota(jnp.int32, (8, length), 0)
    cluster = lax.broadcasted_iota(jnp.int32, (8, length), 1) // LANES
    anchors = [where_ref[0], where_ref[1], where_ref[2]]
    edge_ok = where_ref[3] == 1
    want = jnp.where(line == 0, anchors[0], jnp.where(line == 1, anchors[1], anchors[2]))
    want = jnp.where(line < 3, want, -1)
    qrow_ref[...] = jnp.full(qrow_ref.shape, -2.0, F32)
    krow_ref[...] = jnp.full(krow_ref.shape, -1.0, F32)
    segs, pads = [], []
    for block in range(3):
        start = pl.multiple_of(anchors[block] * LANES, LANES)
        segs.append(row_of(seg_ref[:, pl.ds(start, LANES)], row).astype(F32))
        pads.append(row_of(pad_ref[:, pl.ds(start, LANES)], row))
    for head in range(head_count):
        members = cl_ref[0, head : head + 1, :]
        onehot = (spot == (members % LANES)).astype(F32).astype(BF16)
        chosen = jnp.where((members // LANES) == want, cluster, 0).astype(F32).astype(BF16)
        found = dot_nt(chosen, onehot)
        for block in range(3):
            code = found[block : block + 1, :] * 8.0 + segs[block]
            query, key = code, jnp.where(pads[block] == 1, code, -1.0)
            if block == 2:
                query = jnp.where(edge_ok, query, -2.0)
                key = jnp.where(edge_ok, key, -1.0)
            at = block * 16 + head
            qrow_ref[0, at : at + 1, :] = query
            krow_ref[0, at : at + 1, :] = key
    qrow_ref[0, 48:49, :] = (pads[0] == 1).astype(F32)
    qcol_ref[0] = qrow_ref[0].T
    kcol_ref[0] = krow_ref[0].T


def row_of(block, row):
    chosen = lax.broadcasted_iota(jnp.int32, block.shape, 0) == row
    return jnp.sum(jnp.where(chosen, block, 0), axis=0, keepdims=True)


def cluster_codes(clusters, segment_ids, padding, where_at):
    row_count, head_count, length = clusters.shape
    table = jax.ShapeDtypeStruct((row_count, LANES, LANES), F32)
    spec = pl.BlockSpec((1, LANES, LANES), lambda r, w: (r, 0, 0))
    return pl.pallas_call(
        codes_kernel,
        out_shape=(table,) * 4,
        grid_spec=pltpu.PrefetchScalarGridSpec(
            num_scalar_prefetch=1,
            grid=(row_count,),
            in_specs=[
                pl.BlockSpec((1, head_count, length), lambda r, w: (r, 0, 0)),
                pl.BlockSpec((row_count, length), lambda r, w: (0, 0)),
                pl.BlockSpec((row_count, length), lambda r, w: (0, 0)),
            ],
            out_specs=[spec] * 4,
        ),
        name="codes",
    )(where_at, clusters, segment_ids, padding)


def widen_kernel(*refs):
    for index, ref in enumerate(refs[:-1]):
        refs[-1][index : index + 1, :] = ref[...].astype(F32).reshape(1, ref.shape[0])


def widened(vectors):
    return pl.pallas_call(
        widen_kernel, out_shape=jax.ShapeDtypeStruct((len(vectors),) + vectors[0].shape, F32), name="widen"
    )(*vectors)


def halves(value):
    low = lax.broadcasted_iota(jnp.int32, value.shape, 1) < (LANES // 2)
    zero = jnp.zeros_like(value)
    return jnp.where(low, value, zero), jnp.where(low, zero, value)


def pick(even, odd):
    return jnp.where(lax.broadcasted_iota(jnp.int32, even.shape, 1) < (LANES // 2), even, odd)


def diagonal():
    return lax.broadcasted_iota(jnp.int32, (LANES, LANES), 0) == lax.broadcasted_iota(
        jnp.int32, (LANES, LANES), 1
    )


def attend_kernel(
    model, q_ref, k_ref, v_ref, kc_ref, ke_ref, vc_ref, ve_ref, krow_ref, qcol_ref, ctx_ref, lse_ref, stat_ref
):
    eye = diagonal()
    lane = lax.broadcasted_iota(jnp.int32, (LANES, LANES), 1)
    lse_all = jnp.zeros((LANES, LANES), F32)
    entropy_all = jnp.zeros((LANES, LANES), F32)
    count_all = jnp.ones((LANES, LANES), F32)
    for pair in range(model // LANES):
        at = slice(pair * LANES, (pair + 1) * LANES)
        queries = halves(q_ref[0, :, at])
        keys = jnp.concatenate([r[0, :, at] for r in (k_ref, kc_ref, ke_ref)], axis=0)
        values = jnp.concatenate([r[0, :, at] for r in (v_ref, vc_ref, ve_ref)], axis=0)
        out = []
        for side in range(2):
            head = pair * 2 + side
            raw = dot_nt(queries[side], keys)
            code = qcol_ref[0, :, head : head + 1]
            allowed = [code == krow_ref[0, b * 16 + head : b * 16 + head + 1, :] for b in range(3)]
            allowed[0] = allowed[0] | eye
            allowed = jnp.concatenate(allowed, axis=1)
            masked = jnp.where(allowed, raw, NEGATIVE)
            top = jnp.max(masked, axis=1, keepdims=True)
            grown = jnp.exp(masked - top)
            total = jnp.sum(grown, axis=1, keepdims=True)
            prob = grown * (1.0 / total)
            lse = top + jnp.log(total)
            entropy = lse - jnp.sum(prob * masked, axis=1, keepdims=True)
            count = jnp.sum(jnp.where(allowed, 1.0, 0.0), axis=1, keepdims=True)
            out.append(dot_nn(prob.astype(BF16), values))
            lse_all = jnp.where(lane == head, lse, lse_all)
            entropy_all = jnp.where(lane == head, entropy, entropy_all)
            count_all = jnp.where(lane == head, count, count_all)
        ctx_ref[0, :, at] = pick(out[0], out[1]).astype(BF16)
    real = qcol_ref[0, :, 48:49]
    stat_ref[0] = jnp.zeros(stat_ref.shape[1:], F32)
    stat_ref[0, 0:1, :] = jnp.sum(entropy_all * real, axis=0, keepdims=True)
    stat_ref[0, 1:2, :] = jnp.sum(jnp.log(count_all) * real, axis=0, keepdims=True)
    stat_ref[0, 2:3, :] = jnp.sum(jnp.broadcast_to(real, (LANES, LANES)), axis=0, keepdims=True)
    lse_ref[0] = lse_all.T[:16, :]


def attend(q, k, v, kc, ke, vc, ve, krow, qcol):
    row_count, shard_len, model = q.shape
    own = pl.BlockSpec((1, shard_len, model), lambda r: (r, 0, 0))
    table = pl.BlockSpec((1, LANES, LANES), lambda r: (r, 0, 0))
    return pl.pallas_call(
        lambda *refs: attend_kernel(model, *refs),
        out_shape=(
            jax.ShapeDtypeStruct(q.shape, BF16),
            jax.ShapeDtypeStruct((row_count, 16, LANES), F32),
            jax.ShapeDtypeStruct((row_count, 8, LANES), F32),
        ),
        grid=(row_count,),
        in_specs=[own] * 7 + [table] * 2,
        out_specs=(
            own,
            pl.BlockSpec((1, 16, LANES), lambda r: (r, 0, 0)),
            pl.BlockSpec((1, 8, LANES), lambda r: (r, 0, 0)),
        ),
        name="attend",
    )(q, k, v, kc, ke, vc, ve, krow, qcol)


def pull_query_kernel(
    model, q_ref, k_ref, v_ref, d_ref, kc_ref, ke_ref, vc_ref, ve_ref, row_ref, krow_ref, qcol_ref, out_ref, bias_ref
):
    eye = diagonal()
    cols = jnp.concatenate([row_ref[0], jnp.zeros((LANES - 32, LANES), F32)], axis=0).T
    bias_ref[0] = jnp.zeros(bias_ref.shape[1:], F32)
    for pair in range(model // LANES):
        at = slice(pair * LANES, (pair + 1) * LANES)
        queries, grads = halves(q_ref[0, :, at]), halves(d_ref[0, :, at])
        k_all = jnp.concatenate([r[0, :, at] for r in (k_ref, kc_ref, ke_ref)], axis=0)
        v_all = jnp.concatenate([r[0, :, at] for r in (v_ref, vc_ref, ve_ref)], axis=0)
        dq = []
        for side in range(2):
            head = pair * 2 + side
            code = qcol_ref[0, :, head : head + 1]
            allowed = [code == krow_ref[0, b * 16 + head : b * 16 + head + 1, :] for b in range(3)]
            allowed[0] = allowed[0] | eye
            raw = dot_nt(queries[side], k_all)
            lse, delta = cols[:, head : head + 1], cols[:, 16 + head : 17 + head]
            prob = jnp.exp(jnp.where(jnp.concatenate(allowed, axis=1), raw, NEGATIVE) - lse)
            d_score = (prob * (dot_nt(grads[side], v_all) - delta)).astype(BF16)
            dq.append(dot_nn(d_score, k_all))
        low = pick(dq[0], dq[1]).astype(BF16)
        wide = low.astype(F32) * 0.125
        out_ref[0, :, at] = wide.astype(BF16)
        bias_ref[0, 0:1, at] = jnp.sum(wide, axis=0, keepdims=True)


def pull_pair_kernel(
    model,
    q_ref,
    k_ref,
    v_ref,
    d_ref,
    qc_ref,
    qe_ref,
    dc_ref,
    de_ref,
    row_ref,
    rowc_ref,
    rowe_ref,
    qrow_ref,
    kcol_ref,
    out_ref,
    bias_ref,
):
    eye = diagonal()
    bias_ref[0] = jnp.zeros(bias_ref.shape[1:], F32)
    for pair in range(model // LANES):
        at = slice(pair * LANES, (pair + 1) * LANES)
        keys, values = halves(k_ref[0, :, at]), halves(v_ref[0, :, at])
        q_all = jnp.concatenate([r[0, :, at] for r in (q_ref, qc_ref, qe_ref)], axis=0)
        d_all = jnp.concatenate([r[0, :, at] for r in (d_ref, dc_ref, de_ref)], axis=0)
        dk, dv = [], []
        for side in range(2):
            head = pair * 2 + side
            code = kcol_ref[0, :, head : head + 1]
            allowed = [code == qrow_ref[0, b * 16 + head : b * 16 + head + 1, :] for b in range(3)]
            allowed[0] = allowed[0] | eye
            raw = dot_nt(keys[side], q_all)
            lse = jnp.concatenate([r[0, head : head + 1, :] for r in (row_ref, rowc_ref, rowe_ref)], axis=1)
            delta = jnp.concatenate(
                [r[0, 16 + head : 17 + head, :] for r in (row_ref, rowc_ref, rowe_ref)], axis=1
            )
            prob = jnp.exp(jnp.where(jnp.concatenate(allowed, axis=1), raw, NEGATIVE) - lse)
            d_score = (prob * (dot_nt(values[side], d_all) - delta)).astype(BF16)
            dk.append(dot_nn(d_score, q_all))
            dv.append(dot_nn(prob.astype(BF16), d_all))
        for index, both in enumerate((dk, dv)):
            low = pick(both[0], both[1]).astype(BF16)
            spot = slice(index * model + pair * LANES, index * model + (pair + 1) * LANES)
            out_ref[0, :, spot] = low
            bias_ref[0, 0:1, spot] = jnp.sum(low.astype(F32), axis=0, keepdims=True)


def pull(kernel, copies, activations, lines, tables):
    row_count, shard_len, model = activations[0].shape
    own = pl.BlockSpec((1, shard_len, model), lambda r: (r, 0, 0))
    table = pl.BlockSpec((1, LANES, LANES), lambda r: (r, 0, 0))
    line = pl.BlockSpec((1, 32, LANES), lambda r: (r, 0, 0))
    return pl.pallas_call(
        lambda *refs: kernel(model, *refs),
        out_shape=(
            jax.ShapeDtypeStruct((row_count, shard_len, copies * model), BF16),
            jax.ShapeDtypeStruct((row_count, 8, copies * model), F32),
        ),
        grid=(row_count,),
        in_specs=[own] * len(activations) + [line] * len(lines) + [table] * len(tables),
        out_specs=(
            pl.BlockSpec((1, shard_len, copies * model), lambda r: (r, 0, 0)),
            pl.BlockSpec((1, 8, copies * model), lambda r: (r, 0, 0)),
        ),
    )(*activations, *lines, *tables)


def normed(value):
    centred = value - jnp.mean(value, axis=-1, keepdims=True)
    inverse = lax.rsqrt(jnp.mean(centred * centred, axis=-1, keepdims=True) + EPSILON)
    return centred * inverse, inverse


def norm_pull(grad, gain, unit, inverse):
    scaled = grad * gain
    moved = scaled - jnp.mean(scaled, axis=-1, keepdims=True)
    moved = moved - unit * jnp.mean(scaled * unit, axis=-1, keepdims=True)
    return moved * inverse


def gelu_both(value):
    cdf = 0.5 * (1.0 + lax.erf(value * (0.5**0.5)))
    density = jnp.exp(-0.5 * value * value) * 0.3989422804014327
    return value * cdf, cdf + value * density


class Links:
    def __init__(self, dp_size, seq_size):
        self.dp, self.seq = dp_size, seq_size
        self.dp_at, self.seq_at = lax.axis_index("dp"), lax.axis_index("seq")
        self.bits = [1 << n for n in range(1, dp_size.bit_length() - 1)]

    def swap(self, value, dp_bits, seq_bits):
        pairs = [
            (d * self.seq + s, (d ^ dp_bits) * self.seq + (s ^ seq_bits))
            for d in range(self.dp)
            for s in range(self.seq)
        ]
        return lax.ppermute(value, AXES, pairs)

    def edge(self, value):
        pairs = []
        for d in range(self.dp):
            for s in range(1, self.seq - 1, 2):
                pairs.append((d * self.seq + s, d * self.seq + s + 1))
                pairs.append((d * self.seq + s + 1, d * self.seq + s))
        return lax.ppermute(value, AXES, pairs)

    def dp_stage(self, bit):
        return [(0, 0), (bit, 0)], (self.dp_at // bit) % 2, "x" if bit == 1 else "z%d" % bit

    def y_stage(self):
        return [(0, 0), (0, 2)], self.seq_at // 2, "y"

    def plane(self):
        return [(j & 1, (j >> 1) * 2) for j in range(4)], (self.dp_at % 2) + 2 * (self.seq_at // 2), "p"

    def z_stages(self):
        return [self.dp_stage(bit) for bit in self.bits]

    def wide_z_stages(self):
        stages, stride = [], 2
        while stride < self.dp:
            radix = min(4, self.dp // stride)
            partners = [(j * stride, 0) for j in range(radix)]
            stages.append((partners, (self.dp_at // stride) % radix, "w%d" % stride))
            stride *= radix
        return stages

    def spread(self, value, stage, axis=0):
        partners, mine, _ = stage
        rows = value.shape[axis] // len(partners)
        total = lax.dynamic_slice_in_dim(value, mine * rows, rows, axis).astype(F32)
        for index in range(1, len(partners)):
            sent = lax.dynamic_slice_in_dim(value, (mine ^ index) * rows, rows, axis)
            total = total + self.swap(sent, *partners[index]).astype(F32)
        return total.astype(BF16)

    def collect(self, value, stage, axis=0):
        partners, mine, _ = stage
        pieces = [value]
        for index in range(1, len(partners)):
            pieces.append(self.swap(value, *partners[index]))
        bit = 1
        while bit < len(pieces):
            odd = (mine // bit) % 2 == 1
            pieces = [jnp.where(odd, pieces[n ^ bit], pieces[n]) for n in range(len(pieces))]
            bit *= 2
        return jnp.concatenate(pieces, axis=axis)

    def core_spread(self, value):
        mine = self.seq_at % 2
        cols = value.shape[1] // 2
        keep = lax.dynamic_slice_in_dim(value, mine * cols, cols, 1)
        sent = lax.dynamic_slice_in_dim(value, (1 - mine) * cols, cols, 1)
        return (keep.astype(F32) + self.swap(sent, 0, 1).astype(F32)).astype(BF16)

    def core_collect(self, value):
        mine = self.seq_at % 2
        other = self.swap(value, 0, 1)
        return jnp.where(mine == 0, value, other), jnp.where(mine == 0, other, value)

    def total(self, value):
        for bits in (1, 2):
            value = value + self.swap(value, 0, bits)
        stride = 1
        while stride < self.dp:
            value = value + self.swap(value, stride, 0)
            stride *= 2
        return value

    def around(self, value, stages, axis=0):
        for stage in stages:
            value = self.spread(value, stage, axis)
        for stage in reversed(stages):
            value = self.collect(value, stage, axis)
        return value


def body(
    tokens,
    segment_ids,
    padding,
    clusters,
    w_query,
    w_key,
    w_value,
    w_output,
    b_query,
    b_value,
    b_output,
    gain_attn,
    shift_attn,
    w_inner,
    b_inner,
    w_outer,
    b_outer,
    gain_ffn,
    shift_ffn,
    cotangent,
):
    links = Links(lax.axis_size("dp"), lax.axis_size("seq"))
    seq_at, seq_count = links.seq_at, links.seq
    row_count, shard_len, model = tokens.shape
    head_count = clusters.shape[1]
    amount = row_count * shard_len
    own_shape = (row_count, shard_len, model)
    tokens_edge = links.edge(tokens)
    tokens_core = links.swap(tokens, 0, 1)
    inner, outer, inner_bias = [w_inner], [w_outer], [b_inner[None, :]]
    inner.append(links.swap(w_inner, 0, 2))
    outer.append(links.swap(w_outer, 0, 2))
    inner_bias.append(links.swap(inner_bias[0], 0, 2))
    for index in range(2):
        inner.append(links.swap(inner[index], 0, 1))
        outer.append(links.swap(outer[index], 0, 1))
    both = links.swap(jnp.concatenate(inner_bias, axis=0), 0, 1)
    inner_bias += [both[0:1], both[1:2]]

    line = lax.broadcasted_iota(jnp.int32, (4,), 0)
    edge_raw = jnp.where(seq_at % 2 == 1, seq_at + 1, seq_at - 1)
    edge_ok = (edge_raw >= 0) & (edge_raw < seq_count)
    where_at = jnp.where(line == 2, jnp.clip(edge_raw, 0, seq_count - 1), edge_ok.astype(jnp.int32))
    where_at = jnp.where(line == 0, seq_at, jnp.where(line == 1, seq_at ^ 1, where_at)).astype(jnp.int32)
    qrow, krow, qcol, kcol = cluster_codes(clusters, segment_ids, padding, where_at)
    vectors = [b_query, b_value, b_output, gain_attn, shift_attn, b_outer, gain_ffn, shift_ffn]
    vectors = widened(vectors)
    bias_query, bias_value, bias_output, gain_one, shift_one, bias_outer, gain_two, shift_two = [
        vectors[n : n + 1] for n in range(8)
    ]

    def make_query(array):
        return ((dot_nn(array, w_query) + bias_query) * 0.125).astype(BF16).reshape(own_shape)

    def make_key(array):
        return dot_nn(array, w_key).astype(BF16).reshape(own_shape)

    def make_value(array):
        return (dot_nn(array, w_value) + bias_value).astype(BF16).reshape(own_shape)

    flat = tokens.reshape(amount, model)
    flat_core, flat_edge = tokens_core.reshape(amount, model), tokens_edge.reshape(amount, model)
    q, k, v = make_query(flat), make_key(flat), make_value(flat)
    k_core, v_core = make_key(flat_core), make_value(flat_core)
    k_edge, v_edge = make_key(flat_edge), make_value(flat_edge)
    context, lse, stats = attend(q, k, v, k_core, k_edge, v_core, v_edge, krow, qcol)
    q_core, q_edge = make_query(flat_core), make_query(flat_edge)
    context = context.reshape(amount, model)

    x = flat.astype(F32)
    residual_one = x + dot_nn(context, w_output) + bias_output
    unit_one, inverse_one = normed(residual_one)
    mid = unit_one * gain_one + shift_one
    mid_low = mid.astype(BF16)

    acts, slopes = [None] * 4, [None] * 4
    residual_two = mid + bias_outer
    for index in (0, 2, 1, 3):
        pre = dot_nn(mid_low, inner[index]) + inner_bias[index].astype(F32)
        act, slope = gelu_both(pre)
        acts[index] = act.astype(BF16)
        slopes[index] = slope
        residual_two = residual_two + dot_nn(acts[index], outer[index])
    unit_two, inverse_two = normed(residual_two)
    output = (unit_two * gain_two + shift_two).astype(BF16)
    grad = cotangent.reshape(amount, model).astype(F32)
    d_two = norm_pull(grad, gain_two, unit_two, inverse_two)
    d_two_low = d_two.astype(BF16)

    grads_inner, grads_outer, grads_bias = [None] * 4, [None] * 4, [None] * 4

    def far_of(parts):
        return parts[1] + links.swap(parts[3].astype(BF16), 0, 1).astype(F32)

    def near_of(parts):
        return parts[0] + links.swap(parts[2].astype(BF16), 0, 1).astype(F32)

    for index in (3, 1, 2, 0):
        grads_outer[index] = dot_tn(acts[index], d_two_low)
    far = far_of(grads_outer).astype(BF16)
    near = near_of(grads_outer)
    grad_outer = (near + links.swap(far, 0, 2).astype(F32)).astype(BF16)

    d_mid = d_two
    for index in (0, 2, 1, 3):
        d_pre = (slopes[index] * dot_nt(d_two_low, outer[index])).astype(BF16)
        grads_bias[index] = jnp.sum(d_pre.astype(F32), axis=0)
        d_mid = d_mid + dot_nt(d_pre, inner[index])
        grads_inner[index] = dot_tn(mid_low, d_pre)

    d_one = norm_pull(d_mid, gain_one, unit_one, inverse_one)
    d_one_low = d_one.astype(BF16)
    d_context = dot_nt(d_one_low, w_output).astype(BF16)
    d_context_own = d_context.reshape(own_shape)
    d_edge = links.edge(d_context_own)
    d_core = links.swap(d_context_own, 0, 1)
    head_of = lax.broadcasted_iota(jnp.int32, (16, model), 1) // (model // head_count)
    head_sum = (head_of == lax.broadcasted_iota(jnp.int32, (16, model), 0)).astype(F32)
    delta = lax.dot_general(
        head_sum,
        d_context.astype(F32) * context.astype(F32),
        (((1,), (1,)), ((), ())),
        precision=lax.Precision.HIGHEST,
        preferred_element_type=F32,
    )
    delta = jnp.transpose(delta.reshape(16, row_count, shard_len), (1, 0, 2))
    lines = jnp.concatenate([lse, delta], axis=1)
    lines_edge = links.edge(lines)
    lines_core = links.swap(lines, 0, 1)

    pair = jnp.stack([near_of(grads_inner), far_of(grads_inner)]).astype(BF16)
    pair = links.spread(pair, links.dp_stage(1), 1)
    grad_inner = pair[0].astype(F32) + links.swap(pair[1], 0, 2).astype(F32)
    grad_inner = links.around(grad_inner.astype(BF16), links.z_stages())
    grad_inner = links.collect(grad_inner, links.dp_stage(1)).astype(F32)

    grad_outer = links.spread(grad_outer, links.dp_stage(1))
    grad_outer = links.around(grad_outer, links.z_stages())
    grad_outer = links.collect(grad_outer, links.dp_stage(1)).astype(F32)

    d_query, bias_dq = pull(
        pull_query_kernel, 1, [q, k, v, d_context_own, k_core, k_edge, v_core, v_edge], [lines], [krow, qcol]
    )
    d_query = d_query.reshape(amount, model)
    grad_w_output = dot_tn(context, d_one_low).astype(BF16)
    grad_w_query = dot_tn(flat, d_query).astype(BF16)
    first = jnp.stack([links.core_spread(grad_w_output), links.core_spread(grad_w_query)])
    first = links.around(first, [links.y_stage(), links.dp_stage(1)] + links.z_stages(), 1)
    low, high = links.core_collect(first)
    grad_w_output, grad_w_query = [jnp.concatenate([low[n], high[n]], axis=1).astype(F32) for n in range(2)]

    d_pair, bias_pair = pull(
        pull_pair_kernel,
        2,
        [q, k, v, d_context_own, q_core, q_edge, d_core, d_edge],
        [lines, lines_core, lines_edge],
        [qrow, kcol],
    )
    d_pair = d_pair.reshape(amount, 2 * model)
    last = dot_tn(flat, d_pair).astype(BF16)
    last = links.core_spread(last)
    last = links.around(last, [links.plane()] + links.wide_z_stages())
    grad_w_key, grad_w_value = [half.astype(F32) for half in links.core_collect(last)]

    grad_tokens = (
        d_one
        + dot_nt(d_query, w_query)
        + dot_nt(d_pair[:, :model], w_key)
        + dot_nt(d_pair[:, model:], w_value)
    ).astype(BF16)

    def placed(bits):
        order = [bits[0], bits[2], bits[1], bits[3]]
        stacked = jnp.stack(order)
        return jnp.stack([lax.dynamic_index_in_dim(stacked, seq_at ^ a, 0, False) for a in range(4)])

    stat_rows = jnp.sum(stats, axis=0)[0:3, :]
    stat_rows = jnp.pad(stat_rows, ((0, 0), (0, model - LANES)))
    small = [jnp.sum(bias_dq[:, 0:1, :], axis=0), jnp.sum(bias_pair[:, 0:1, model:], axis=0)]
    small += [
        jnp.sum(value, axis=0, keepdims=True)
        for value in (d_one, d_mid * unit_one, d_mid, d_two, grad * unit_two, grad)
    ]
    small = links.total(jnp.concatenate(small + [stat_rows, placed(grads_bias)], axis=0))
    cluster_log = small[8:10, :head_count] / small[10:11, 0:1]
    return (
        output.reshape(own_shape),
        grad_tokens.reshape(own_shape),
        grad_w_query,
        grad_w_key,
        grad_w_value,
        grad_w_output,
        small[0],
        small[1],
        small[2],
        small[3],
        small[4],
        grad_inner,
        lax.dynamic_index_in_dim(small[11:15], seq_at, 0, False),
        grad_outer,
        small[5],
        small[6],
        small[7],
        cluster_log,
    )


def solution(mesh):
    return jax.shard_map(
        body,
        mesh=mesh,
        in_specs=(
            P("dp", "seq", None),
            P("dp", None),
            P("dp", None),
            P("dp", None, None),
            P(),
            P(),
            P(),
            P(),
            P(),
            P(),
            P(),
            P(),
            P(),
            P(None, "seq"),
            P("seq"),
            P("seq", None),
            P(),
            P(),
            P(),
            P("dp", "seq", None),
        ),
        out_specs=(
            P("dp", "seq", None),
            P("dp", "seq", None),
            P(),
            P(),
            P(),
            P(),
            P(),
            P(),
            P(),
            P(),
            P(),
            P(None, "seq"),
            P("seq"),
            P("seq", None),
            P(),
            P(),
            P(),
            P(),
        ),
        check_vma=False,
    )
```

```python
import jax
import jax.numpy as jnp
from jax import lax
from jax.experimental import pallas as pl
from jax.experimental.pallas import tpu as pltpu
from jax.sharding import PartitionSpec as P


EPSILON = 1e-12
NEGATIVE = -1e30
LANES = 128
AXES = ("dp", "seq")
F32 = jnp.float32
BF16 = jnp.bfloat16


def dot_nn(left, right):
    return lax.dot_general(left, right, (((1,), (0,)), ((), ())), preferred_element_type=F32)


def dot_nt(left, right):
    return lax.dot_general(left, right, (((1,), (1,)), ((), ())), preferred_element_type=F32)


def dot_tn(left, right):
    return lax.dot_general(left, right, (((0,), (0,)), ((), ())), preferred_element_type=F32)


def codes_kernel(where_ref, cl_ref, seg_ref, pad_ref, qrow_ref, krow_ref, qcol_ref, kcol_ref):
    row = pl.program_id(0)
    head_count = cl_ref.shape[1]
    length = cl_ref.shape[2]
    spot = lax.broadcasted_iota(jnp.int32, (LANES, length), 0)
    line = lax.broadcasted_iota(jnp.int32, (8, length), 0)
    cluster = lax.broadcasted_iota(jnp.int32, (8, length), 1) // LANES
    anchors = [where_ref[0], where_ref[1], where_ref[2]]
    edge_ok = where_ref[3] == 1
    want = jnp.where(line == 0, anchors[0], jnp.where(line == 1, anchors[1], anchors[2]))
    want = jnp.where(line < 3, want, -1)
    qrow_ref[...] = jnp.full(qrow_ref.shape, -2.0, F32)
    krow_ref[...] = jnp.full(krow_ref.shape, -1.0, F32)
    segs, pads = [], []
    for block in range(3):
        start = pl.multiple_of(anchors[block] * LANES, LANES)
        segs.append(row_of(seg_ref[:, pl.ds(start, LANES)], row).astype(F32))
        pads.append(row_of(pad_ref[:, pl.ds(start, LANES)], row))
    for head in range(head_count):
        members = cl_ref[0, head : head + 1, :]
        onehot = (spot == (members % LANES)).astype(F32).astype(BF16)
        chosen = jnp.where((members // LANES) == want, cluster, 0).astype(F32).astype(BF16)
        found = dot_nt(chosen, onehot)
        for block in range(3):
            code = found[block : block + 1, :] * 8.0 + segs[block]
            query, key = code, jnp.where(pads[block] == 1, code, -1.0)
            if block == 2:
                query = jnp.where(edge_ok, query, -2.0)
                key = jnp.where(edge_ok, key, -1.0)
            at = block * 16 + head
            qrow_ref[0, at : at + 1, :] = query
            krow_ref[0, at : at + 1, :] = key
    qrow_ref[0, 48:49, :] = (pads[0] == 1).astype(F32)
    qcol_ref[0] = qrow_ref[0].T
    kcol_ref[0] = krow_ref[0].T


def row_of(block, row):
    chosen = lax.broadcasted_iota(jnp.int32, block.shape, 0) == row
    return jnp.sum(jnp.where(chosen, block, 0), axis=0, keepdims=True)


def cluster_codes(clusters, segment_ids, padding, where_at):
    row_count, head_count, length = clusters.shape
    table = jax.ShapeDtypeStruct((row_count, LANES, LANES), F32)
    spec = pl.BlockSpec((1, LANES, LANES), lambda r, w: (r, 0, 0))
    return pl.pallas_call(
        codes_kernel,
        out_shape=(table,) * 4,
        grid_spec=pltpu.PrefetchScalarGridSpec(
            num_scalar_prefetch=1,
            grid=(row_count,),
            in_specs=[
                pl.BlockSpec((1, head_count, length), lambda r, w: (r, 0, 0)),
                pl.BlockSpec((row_count, length), lambda r, w: (0, 0)),
                pl.BlockSpec((row_count, length), lambda r, w: (0, 0)),
            ],
            out_specs=[spec] * 4,
        ),
        name="codes",
    )(where_at, clusters, segment_ids, padding)


def widen_kernel(*refs):
    for index, ref in enumerate(refs[:-1]):
        refs[-1][index : index + 1, :] = ref[...].astype(F32).reshape(1, ref.shape[0])


def widened(vectors):
    return pl.pallas_call(
        widen_kernel, out_shape=jax.ShapeDtypeStruct((len(vectors),) + vectors[0].shape, F32), name="widen"
    )(*vectors)


def halves(value):
    low = lax.broadcasted_iota(jnp.int32, value.shape, 1) < (LANES // 2)
    zero = jnp.zeros_like(value)
    return jnp.where(low, value, zero), jnp.where(low, zero, value)


def pick(even, odd):
    return jnp.where(lax.broadcasted_iota(jnp.int32, even.shape, 1) < (LANES // 2), even, odd)


def diagonal():
    return lax.broadcasted_iota(jnp.int32, (LANES, LANES), 0) == lax.broadcasted_iota(
        jnp.int32, (LANES, LANES), 1
    )


def attend_kernel(
    model, q_ref, k_ref, v_ref, kc_ref, ke_ref, vc_ref, ve_ref, krow_ref, qcol_ref, ctx_ref, lse_ref, stat_ref
):
    eye = diagonal()
    lane = lax.broadcasted_iota(jnp.int32, (LANES, LANES), 1)
    lse_all = jnp.zeros((LANES, LANES), F32)
    entropy_all = jnp.zeros((LANES, LANES), F32)
    count_all = jnp.ones((LANES, LANES), F32)
    for pair in range(model // LANES):
        at = slice(pair * LANES, (pair + 1) * LANES)
        queries = halves(q_ref[0, :, at])
        keys = jnp.concatenate([r[0, :, at] for r in (k_ref, kc_ref, ke_ref)], axis=0)
        values = jnp.concatenate([r[0, :, at] for r in (v_ref, vc_ref, ve_ref)], axis=0)
        out = []
        for side in range(2):
            head = pair * 2 + side
            raw = dot_nt(queries[side], keys)
            code = qcol_ref[0, :, head : head + 1]
            allowed = [code == krow_ref[0, b * 16 + head : b * 16 + head + 1, :] for b in range(3)]
            allowed[0] = allowed[0] | eye
            allowed = jnp.concatenate(allowed, axis=1)
            masked = jnp.where(allowed, raw, NEGATIVE)
            top = jnp.max(masked, axis=1, keepdims=True)
            grown = jnp.exp(masked - top)
            total = jnp.sum(grown, axis=1, keepdims=True)
            prob = grown * (1.0 / total)
            lse = top + jnp.log(total)
            entropy = lse - jnp.sum(prob * masked, axis=1, keepdims=True)
            count = jnp.sum(jnp.where(allowed, 1.0, 0.0), axis=1, keepdims=True)
            out.append(dot_nn(prob.astype(BF16), values))
            lse_all = jnp.where(lane == head, lse, lse_all)
            entropy_all = jnp.where(lane == head, entropy, entropy_all)
            count_all = jnp.where(lane == head, count, count_all)
        ctx_ref[0, :, at] = pick(out[0], out[1]).astype(BF16)
    real = qcol_ref[0, :, 48:49]
    stat_ref[0] = jnp.zeros(stat_ref.shape[1:], F32)
    stat_ref[0, 0:1, :] = jnp.sum(entropy_all * real, axis=0, keepdims=True)
    stat_ref[0, 1:2, :] = jnp.sum(jnp.log(count_all) * real, axis=0, keepdims=True)
    stat_ref[0, 2:3, :] = jnp.sum(jnp.broadcast_to(real, (LANES, LANES)), axis=0, keepdims=True)
    lse_ref[0] = lse_all.T[:16, :]


def attend(q, k, v, kc, ke, vc, ve, krow, qcol):
    row_count, shard_len, model = q.shape
    own = pl.BlockSpec((1, shard_len, model), lambda r: (r, 0, 0))
    table = pl.BlockSpec((1, LANES, LANES), lambda r: (r, 0, 0))
    return pl.pallas_call(
        lambda *refs: attend_kernel(model, *refs),
        out_shape=(
            jax.ShapeDtypeStruct(q.shape, BF16),
            jax.ShapeDtypeStruct((row_count, 16, LANES), F32),
            jax.ShapeDtypeStruct((row_count, 8, LANES), F32),
        ),
        grid=(row_count,),
        in_specs=[own] * 7 + [table] * 2,
        out_specs=(
            own,
            pl.BlockSpec((1, 16, LANES), lambda r: (r, 0, 0)),
            pl.BlockSpec((1, 8, LANES), lambda r: (r, 0, 0)),
        ),
        name="attend",
    )(q, k, v, kc, ke, vc, ve, krow, qcol)


def pull_query_kernel(
    model, q_ref, k_ref, v_ref, d_ref, kc_ref, ke_ref, vc_ref, ve_ref, row_ref, krow_ref, qcol_ref, out_ref, bias_ref
):
    eye = diagonal()
    cols = jnp.concatenate([row_ref[0], jnp.zeros((LANES - 32, LANES), F32)], axis=0).T
    bias_ref[0] = jnp.zeros(bias_ref.shape[1:], F32)
    for pair in range(model // LANES):
        at = slice(pair * LANES, (pair + 1) * LANES)
        queries, grads = halves(q_ref[0, :, at]), halves(d_ref[0, :, at])
        k_all = jnp.concatenate([r[0, :, at] for r in (k_ref, kc_ref, ke_ref)], axis=0)
        v_all = jnp.concatenate([r[0, :, at] for r in (v_ref, vc_ref, ve_ref)], axis=0)
        dq = []
        for side in range(2):
            head = pair * 2 + side
            code = qcol_ref[0, :, head : head + 1]
            allowed = [code == krow_ref[0, b * 16 + head : b * 16 + head + 1, :] for b in range(3)]
            allowed[0] = allowed[0] | eye
            raw = dot_nt(queries[side], k_all)
            lse, delta = cols[:, head : head + 1], cols[:, 16 + head : 17 + head]
            prob = jnp.exp(jnp.where(jnp.concatenate(allowed, axis=1), raw, NEGATIVE) - lse)
            d_score = (prob * (dot_nt(grads[side], v_all) - delta)).astype(BF16)
            dq.append(dot_nn(d_score, k_all))
        low = pick(dq[0], dq[1]).astype(BF16)
        wide = low.astype(F32) * 0.125
        out_ref[0, :, at] = wide.astype(BF16)
        bias_ref[0, 0:1, at] = jnp.sum(wide, axis=0, keepdims=True)


def pull_pair_kernel(
    model,
    q_ref,
    k_ref,
    v_ref,
    d_ref,
    qc_ref,
    qe_ref,
    dc_ref,
    de_ref,
    row_ref,
    rowc_ref,
    rowe_ref,
    qrow_ref,
    kcol_ref,
    out_ref,
    bias_ref,
):
    eye = diagonal()
    bias_ref[0] = jnp.zeros(bias_ref.shape[1:], F32)
    for pair in range(model // LANES):
        at = slice(pair * LANES, (pair + 1) * LANES)
        keys, values = halves(k_ref[0, :, at]), halves(v_ref[0, :, at])
        q_all = jnp.concatenate([r[0, :, at] for r in (q_ref, qc_ref, qe_ref)], axis=0)
        d_all = jnp.concatenate([r[0, :, at] for r in (d_ref, dc_ref, de_ref)], axis=0)
        dk, dv = [], []
        for side in range(2):
            head = pair * 2 + side
            code = kcol_ref[0, :, head : head + 1]
            allowed = [code == qrow_ref[0, b * 16 + head : b * 16 + head + 1, :] for b in range(3)]
            allowed[0] = allowed[0] | eye
            raw = dot_nt(keys[side], q_all)
            lse = jnp.concatenate([r[0, head : head + 1, :] for r in (row_ref, rowc_ref, rowe_ref)], axis=1)
            delta = jnp.concatenate(
                [r[0, 16 + head : 17 + head, :] for r in (row_ref, rowc_ref, rowe_ref)], axis=1
            )
            prob = jnp.exp(jnp.where(jnp.concatenate(allowed, axis=1), raw, NEGATIVE) - lse)
            d_score = (prob * (dot_nt(values[side], d_all) - delta)).astype(BF16)
            dk.append(dot_nn(d_score, q_all))
            dv.append(dot_nn(prob.astype(BF16), d_all))
        for index, both in enumerate((dk, dv)):
            low = pick(both[0], both[1]).astype(BF16)
            spot = slice(index * model + pair * LANES, index * model + (pair + 1) * LANES)
            out_ref[0, :, spot] = low
            bias_ref[0, 0:1, spot] = jnp.sum(low.astype(F32), axis=0, keepdims=True)


def pull(kernel, copies, activations, lines, tables):
    row_count, shard_len, model = activations[0].shape
    own = pl.BlockSpec((1, shard_len, model), lambda r: (r, 0, 0))
    table = pl.BlockSpec((1, LANES, LANES), lambda r: (r, 0, 0))
    line = pl.BlockSpec((1, 32, LANES), lambda r: (r, 0, 0))
    return pl.pallas_call(
        lambda *refs: kernel(model, *refs),
        out_shape=(
            jax.ShapeDtypeStruct((row_count, shard_len, copies * model), BF16),
            jax.ShapeDtypeStruct((row_count, 8, copies * model), F32),
        ),
        grid=(row_count,),
        in_specs=[own] * len(activations) + [line] * len(lines) + [table] * len(tables),
        out_specs=(
            pl.BlockSpec((1, shard_len, copies * model), lambda r: (r, 0, 0)),
            pl.BlockSpec((1, 8, copies * model), lambda r: (r, 0, 0)),
        ),
    )(*activations, *lines, *tables)


def normed(value):
    centred = value - jnp.mean(value, axis=-1, keepdims=True)
    inverse = lax.rsqrt(jnp.mean(centred * centred, axis=-1, keepdims=True) + EPSILON)
    return centred * inverse, inverse


def norm_pull(grad, gain, unit, inverse):
    scaled = grad * gain
    moved = scaled - jnp.mean(scaled, axis=-1, keepdims=True)
    moved = moved - unit * jnp.mean(scaled * unit, axis=-1, keepdims=True)
    return moved * inverse


def gelu_both(value):
    cdf = 0.5 * (1.0 + lax.erf(value * (0.5**0.5)))
    return value * cdf, cdf + value * (jnp.exp(-0.5 * value * value) * 0.3989422804014327)


CHUNK = 16
ORDER = (0, 2, 1, 3)


def back_kernel(
    low_ref,
    d_two_ref,
    res_ref,
    gain_ref,
    ctx_ref,
    lse_ref,
    out_hbm,
    slope_hbm,
    outer_hbm,
    inner_hbm,
    d_pre_ref,
    d_one_ref,
    d_one_low_ref,
    d_ctx_ref,
    line_ref,
    sum_ref,
    out_buf,
    slope_buf,
    outer_buf,
    inner_buf,
    work_ref,
    mid_ref,
    sems,
):
    amount, model = low_ref.shape
    moves = [None] * 13
    for index in ORDER:
        parts = ((outer_hbm, outer_buf), (slope_hbm, slope_buf), (inner_hbm, inner_buf))
        for kind, (source, target) in enumerate(parts):
            at = kind * 4 + index
            moves[at] = pltpu.make_async_copy(source[index], target.at[index], sems.at[at])
            moves[at].start()
    moves[12] = pltpu.make_async_copy(out_hbm, out_buf, sems.at[12])
    moves[12].start()
    steps = amount // CHUNK
    zero = jnp.zeros((8, model), F32)

    def folded(value):
        return value[:8] + value[8:]

    sum_ref[...] = zero
    for turn, index in enumerate(ORDER):
        moves[index].wait()
        moves[4 + index].wait()
        work_ref[...] = dot_nt(low_ref[...], outer_buf[index])

        def scale(step, total, index=index):
            rows = pl.ds(pl.multiple_of(step * CHUNK, CHUNK), CHUNK)
            value = (slope_buf[index, rows, :] * work_ref[rows, :]).astype(BF16)
            d_pre_ref[index, rows, :] = value
            return total + folded(value.astype(F32))

        total = lax.fori_loop(0, steps, scale, zero)
        sum_ref[index : index + 1, :] = jnp.sum(total, axis=0, keepdims=True)
        moves[8 + index].wait()
        pulled = dot_nt(d_pre_ref[index], inner_buf[index])
        mid_ref[...] = (d_two_ref[...] if turn == 0 else mid_ref[...]) + pulled

    def norm(step, totals):
        rows = pl.ds(pl.multiple_of(step * CHUNK, CHUNK), CHUNK)
        unit, inverse = normed(res_ref[rows, :])
        d_mid = mid_ref[rows, :]
        d_one = norm_pull(d_mid, gain_ref[...], unit, inverse)
        d_one_ref[rows, :] = d_one
        d_one_low_ref[rows, :] = d_one.astype(BF16)
        news = (d_one, d_mid * unit, d_mid)
        return tuple(total + folded(new) for total, new in zip(totals, news))

    totals = lax.fori_loop(0, steps, norm, (zero,) * 3)
    for index, total in enumerate(totals):
        sum_ref[4 + index : 5 + index, :] = jnp.sum(total, axis=0, keepdims=True)
    moves[12].wait()
    d_ctx_ref[...] = dot_nt(d_one_low_ref[...], out_buf[...]).astype(BF16)
    heads = (16, model)
    head_count = 2 * model // LANES
    head_of = lax.broadcasted_iota(jnp.int32, heads, 1) // (model // head_count)
    head_sum = (head_of == lax.broadcasted_iota(jnp.int32, heads, 0)).astype(F32)
    for row in range(amount // LANES):
        rows = slice(row * LANES, (row + 1) * LANES)
        line_ref[row, 0:16, :] = lse_ref[row]
        line_ref[row, 16:32, :] = lax.dot_general(
            head_sum,
            d_ctx_ref[rows, :].astype(F32) * ctx_ref[rows, :].astype(F32),
            (((1,), (1,)), ((), ())),
            precision=lax.Precision.HIGHEST,
            preferred_element_type=F32,
        )


def back(low, d_two, residual, gain, context, lse, w_output, slopes, outer, inner):
    amount, model = low.shape
    here = pl.BlockSpec(memory_space=pltpu.VMEM)
    there = pl.BlockSpec(memory_space=pl.ANY)
    square = (4, model, model)
    return pl.pallas_call(
        lambda *refs: back_kernel(
            *refs[:7], refs[7:11], refs[11:15], refs[15:19], *refs[19:]
        ),
        out_shape=(
            jax.ShapeDtypeStruct((4, amount, model), BF16),
            jax.ShapeDtypeStruct((amount, model), F32),
            jax.ShapeDtypeStruct((amount, model), BF16),
            jax.ShapeDtypeStruct((amount, model), BF16),
            jax.ShapeDtypeStruct((amount // LANES, 32, LANES), F32),
            jax.ShapeDtypeStruct((8, model), F32),
        ),
        in_specs=[here] * 6 + [there] * 13,
        out_specs=(here,) * 6,
        scratch_shapes=[
            pltpu.VMEM((model, model), BF16),
            pltpu.VMEM((4, amount, model), F32),
            pltpu.VMEM(square, BF16),
            pltpu.VMEM(square, BF16),
            pltpu.VMEM((amount, model), F32),
            pltpu.VMEM((amount, model), F32),
            pltpu.SemaphoreType.DMA((13,)),
        ],
        name="back",
    )(low, d_two, residual, gain, context, lse, w_output, *slopes, *outer, *inner)


class Links:
    def __init__(self, dp_size, seq_size):
        self.dp, self.seq = dp_size, seq_size
        self.dp_at, self.seq_at = lax.axis_index("dp"), lax.axis_index("seq")
        self.bits = [1 << n for n in range(1, dp_size.bit_length() - 1)]

    def swap(self, value, dp_bits, seq_bits):
        pairs = [
            (d * self.seq + s, (d ^ dp_bits) * self.seq + (s ^ seq_bits))
            for d in range(self.dp)
            for s in range(self.seq)
        ]
        return lax.ppermute(value, AXES, pairs)

    def edge(self, value):
        pairs = []
        for d in range(self.dp):
            for s in range(1, self.seq - 1, 2):
                pairs.append((d * self.seq + s, d * self.seq + s + 1))
                pairs.append((d * self.seq + s + 1, d * self.seq + s))
        return lax.ppermute(value, AXES, pairs)

    def dp_stage(self, bit):
        return [(0, 0), (bit, 0)], (self.dp_at // bit) % 2, "x" if bit == 1 else "z%d" % bit

    def y_stage(self):
        return [(0, 0), (0, 2)], self.seq_at // 2, "y"

    def plane(self):
        return [(j & 1, (j >> 1) * 2) for j in range(4)], (self.dp_at % 2) + 2 * (self.seq_at // 2), "p"

    def z_stages(self):
        return [self.dp_stage(bit) for bit in self.bits]

    def spread(self, value, stage, axis=0):
        partners, mine, _ = stage
        rows = value.shape[axis] // len(partners)
        total = lax.dynamic_slice_in_dim(value, mine * rows, rows, axis).astype(F32)
        for index in range(1, len(partners)):
            sent = lax.dynamic_slice_in_dim(value, (mine ^ index) * rows, rows, axis)
            total = total + self.swap(sent, *partners[index]).astype(F32)
        return total.astype(BF16)

    def collect(self, value, stage, axis=0):
        partners, mine, _ = stage
        pieces = [value]
        for index in range(1, len(partners)):
            pieces.append(self.swap(value, *partners[index]))
        bit = 1
        while bit < len(pieces):
            odd = (mine // bit) % 2 == 1
            pieces = [jnp.where(odd, pieces[n ^ bit], pieces[n]) for n in range(len(pieces))]
            bit *= 2
        return jnp.concatenate(pieces, axis=axis)

    def core_spread(self, value):
        mine = self.seq_at % 2
        cols = value.shape[1] // 2
        keep = lax.dynamic_slice_in_dim(value, mine * cols, cols, 1)
        sent = lax.dynamic_slice_in_dim(value, (1 - mine) * cols, cols, 1)
        return (keep.astype(F32) + self.swap(sent, 0, 1).astype(F32)).astype(BF16)

    def core_collect(self, value):
        mine = self.seq_at % 2
        other = self.swap(value, 0, 1)
        return jnp.where(mine == 0, value, other), jnp.where(mine == 0, other, value)

    def total(self, value):
        for bits in (1, 2):
            value = value + self.swap(value, 0, bits)
        stride = 1
        while stride < self.dp:
            value = value + self.swap(value, stride, 0)
            stride *= 2
        return value

    def doubled(self, value):
        for bit in self.bits:
            other = self.swap(value, bit, 0)
            value = (value.astype(F32) + other.astype(F32)).astype(BF16)
        return value

    def around(self, value, stages, axis=0):
        for stage in stages:
            value = self.spread(value, stage, axis)
        for stage in reversed(stages):
            value = self.collect(value, stage, axis)
        return value


def body(
    tokens,
    segment_ids,
    padding,
    clusters,
    w_query,
    w_key,
    w_value,
    w_output,
    b_query,
    b_value,
    b_output,
    gain_attn,
    shift_attn,
    w_inner,
    b_inner,
    w_outer,
    b_outer,
    gain_ffn,
    shift_ffn,
    cotangent,
):
    links = Links(lax.axis_size("dp"), lax.axis_size("seq"))
    seq_at, seq_count = links.seq_at, links.seq
    row_count, shard_len, model = tokens.shape
    head_count = clusters.shape[1]
    amount = row_count * shard_len
    own_shape = (row_count, shard_len, model)
    tokens_edge = links.edge(tokens)
    tokens_core = links.swap(tokens, 0, 1)
    inner, outer, inner_bias = [w_inner], [w_outer], [b_inner[None, :]]
    inner.append(links.swap(w_inner, 0, 2))
    outer.append(links.swap(w_outer, 0, 2))
    inner_bias.append(links.swap(inner_bias[0], 0, 2))
    for index in range(2):
        inner.append(links.swap(inner[index], 0, 1))
        outer.append(links.swap(outer[index], 0, 1))
    both = links.swap(jnp.concatenate(inner_bias, axis=0), 0, 1)
    inner_bias += [both[0:1], both[1:2]]

    line = lax.broadcasted_iota(jnp.int32, (4,), 0)
    edge_raw = jnp.where(seq_at % 2 == 1, seq_at + 1, seq_at - 1)
    edge_ok = (edge_raw >= 0) & (edge_raw < seq_count)
    where_at = jnp.where(line == 2, jnp.clip(edge_raw, 0, seq_count - 1), edge_ok.astype(jnp.int32))
    where_at = jnp.where(line == 0, seq_at, jnp.where(line == 1, seq_at ^ 1, where_at)).astype(jnp.int32)
    qrow, krow, qcol, kcol = cluster_codes(clusters, segment_ids, padding, where_at)
    vectors = [b_query, b_value, b_output, gain_attn, shift_attn, b_outer, gain_ffn, shift_ffn]
    vectors = widened(vectors)
    bias_query, bias_value, bias_output, gain_one, shift_one, bias_outer, gain_two, shift_two = [
        vectors[n : n + 1] for n in range(8)
    ]

    def make_query(array):
        return ((dot_nn(array, w_query) + bias_query) * 0.125).astype(BF16).reshape(own_shape)

    def make_key(array):
        return dot_nn(array, w_key).astype(BF16).reshape(own_shape)

    def make_value(array):
        return (dot_nn(array, w_value) + bias_value).astype(BF16).reshape(own_shape)

    flat = tokens.reshape(amount, model)
    flat_core, flat_edge = tokens_core.reshape(amount, model), tokens_edge.reshape(amount, model)
    q, k, v = make_query(flat), make_key(flat), make_value(flat)
    k_core, v_core = make_key(flat_core), make_value(flat_core)
    k_edge, v_edge = make_key(flat_edge), make_value(flat_edge)
    context, lse, stats = attend(q, k, v, k_core, k_edge, v_core, v_edge, krow, qcol)
    q_core, q_edge = make_query(flat_core), make_query(flat_edge)
    context = context.reshape(amount, model)

    x = flat.astype(F32)
    residual_one = x + dot_nn(context, w_output) + bias_output
    unit_one, _ = normed(residual_one)
    mid = unit_one * gain_one + shift_one
    mid_low = mid.astype(BF16)

    acts, slopes = [None] * 4, [None] * 4
    residual_two = mid + bias_outer
    for index in (0, 2, 1, 3):
        act, slopes[index] = gelu_both(dot_nn(mid_low, inner[index]) + inner_bias[index].astype(F32))
        acts[index] = act.astype(BF16)
        residual_two = residual_two + dot_nn(acts[index], outer[index])
    unit_two, inverse_two = normed(residual_two)
    output = (unit_two * gain_two + shift_two).astype(BF16)
    grad = cotangent.reshape(amount, model).astype(F32)
    d_two = norm_pull(grad, gain_two, unit_two, inverse_two)
    d_two_low = d_two.astype(BF16)

    grads_inner, grads_outer = [None] * 4, [None] * 4

    def far_of(parts):
        return parts[1] + links.swap(parts[3].astype(BF16), 0, 1).astype(F32)

    def near_of(parts):
        return parts[0] + links.swap(parts[2].astype(BF16), 0, 1).astype(F32)

    for index in (3, 1, 2, 0):
        grads_outer[index] = dot_tn(acts[index], d_two_low)
    far = far_of(grads_outer).astype(BF16)
    near = near_of(grads_outer)
    grad_outer = (near + links.swap(far, 0, 2).astype(F32)).astype(BF16)

    d_pre, d_one, d_one_low, d_context, lines, sums = back(
        d_two_low, d_two, residual_one, gain_one, context, lse, w_output, slopes, outer, inner
    )
    for index in (3, 1, 2, 0):
        grads_inner[index] = dot_tn(mid_low, d_pre[index])
    d_context_own = d_context.reshape(own_shape)
    d_edge = links.edge(d_context_own)
    d_core = links.swap(d_context_own, 0, 1)
    lines_edge = links.edge(lines)
    lines_core = links.swap(lines, 0, 1)

    pair = jnp.stack([near_of(grads_inner), far_of(grads_inner)]).astype(BF16)
    pair = links.spread(pair, links.dp_stage(1), 1)
    grad_inner = pair[0].astype(F32) + links.swap(pair[1], 0, 2).astype(F32)
    grad_inner = links.around(grad_inner.astype(BF16), links.z_stages())
    grad_inner = links.collect(grad_inner, links.dp_stage(1)).astype(F32)

    grad_outer = links.spread(grad_outer, links.dp_stage(1))
    grad_outer = links.around(grad_outer, links.z_stages())
    grad_outer = links.collect(grad_outer, links.dp_stage(1)).astype(F32)

    d_query, bias_dq = pull(
        pull_query_kernel, 1, [q, k, v, d_context_own, k_core, k_edge, v_core, v_edge], [lines], [krow, qcol]
    )
    d_query = d_query.reshape(amount, model)
    grad_w_output = dot_tn(context, d_one_low).astype(BF16)
    grad_w_query = dot_tn(flat, d_query).astype(BF16)
    first = jnp.stack([links.core_spread(grad_w_output), links.core_spread(grad_w_query)])
    for stage in (links.y_stage(), links.dp_stage(1)):
        first = links.spread(first, stage, 1)
    first = links.doubled(first)
    for stage in (links.dp_stage(1), links.y_stage()):
        first = links.collect(first, stage, 1)
    low, high = links.core_collect(first)
    grad_w_output, grad_w_query = [jnp.concatenate([low[n], high[n]], axis=1).astype(F32) for n in range(2)]

    d_pair, bias_pair = pull(
        pull_pair_kernel,
        2,
        [q, k, v, d_context_own, q_core, q_edge, d_core, d_edge],
        [lines, lines_core, lines_edge],
        [qrow, kcol],
    )
    d_pair = d_pair.reshape(amount, 2 * model)
    last = dot_tn(flat, d_pair).astype(BF16)
    last = links.core_spread(last)
    last = links.spread(last, links.plane())
    last = links.doubled(last)
    last = links.collect(last, links.plane())
    grad_w_key, grad_w_value = [half.astype(F32) for half in links.core_collect(last)]

    grad_tokens = (
        d_one
        + dot_nt(d_query, w_query)
        + dot_nt(d_pair[:, :model], w_key)
        + dot_nt(d_pair[:, model:], w_value)
    ).astype(BF16)

    bias_rows = [sums[0:1], sums[2:3], sums[1:2], sums[3:4]]
    for bit in (1, 2):
        odd = (seq_at // bit) % 2 == 1
        bias_rows = [jnp.where(odd, bias_rows[n ^ bit], bias_rows[n]) for n in range(4)]
    stat_rows = jnp.sum(stats, axis=0)[0:3, :]
    stat_rows = jnp.pad(stat_rows, ((0, 0), (0, model - LANES)))
    small = [jnp.sum(bias_dq[:, 0:1, :], axis=0), jnp.sum(bias_pair[:, 0:1, model:], axis=0), sums[4:7]]
    small += [jnp.sum(value, axis=0, keepdims=True) for value in (d_two, grad * unit_two, grad)]
    small += [stat_rows] + bias_rows
    small = links.total(jnp.concatenate(small, axis=0))
    cluster_log = small[8:10, :head_count] / small[10:11, 0:1]
    return (
        output.reshape(own_shape),
        grad_tokens.reshape(own_shape),
        grad_w_query,
        grad_w_key,
        grad_w_value,
        grad_w_output,
        small[0],
        small[1],
        small[2],
        small[3],
        small[4],
        grad_inner,
        lax.dynamic_index_in_dim(small[11:15], seq_at, 0, False),
        grad_outer,
        small[5],
        small[6],
        small[7],
        cluster_log,
    )


def solution(mesh):
    return jax.shard_map(
        body,
        mesh=mesh,
        in_specs=(
            P("dp", "seq", None),
            P("dp", None),
            P("dp", None),
            P("dp", None, None),
            P(),
            P(),
            P(),
            P(),
            P(),
            P(),
            P(),
            P(),
            P(),
            P(None, "seq"),
            P("seq"),
            P("seq", None),
            P(),
            P(),
            P(),
            P("dp", "seq", None),
        ),
        out_specs=(
            P("dp", "seq", None),
            P("dp", "seq", None),
            P(),
            P(),
            P(),
            P(),
            P(),
            P(),
            P(),
            P(),
            P(),
            P(None, "seq"),
            P("seq"),
            P("seq", None),
            P(),
            P(),
            P(),
            P(),
        ),
        check_vma=False,
    )
```

```python
import jax
import jax.numpy as jnp
from jax import lax
from jax.experimental import pallas as pl
from jax.experimental.pallas import tpu as pltpu
from jax.sharding import PartitionSpec as P


EPSILON = 1e-12
NEGATIVE = -1e30
LANES = 128
AXES = ("dp", "seq")
F32 = jnp.float32
BF16 = jnp.bfloat16


def dot_nn(left, right):
    return lax.dot_general(left, right, (((1,), (0,)), ((), ())), preferred_element_type=F32)


def dot_nt(left, right):
    return lax.dot_general(left, right, (((1,), (1,)), ((), ())), preferred_element_type=F32)


def dot_tn(left, right):
    return lax.dot_general(left, right, (((0,), (0,)), ((), ())), preferred_element_type=F32)


def codes_kernel(where_ref, cl_ref, seg_ref, pad_ref, qrow_ref, krow_ref, qcol_ref, kcol_ref):
    row = pl.program_id(0)
    head_count = cl_ref.shape[1]
    length = cl_ref.shape[2]
    spot = lax.broadcasted_iota(jnp.int32, (LANES, length), 0)
    line = lax.broadcasted_iota(jnp.int32, (8, length), 0)
    cluster = lax.broadcasted_iota(jnp.int32, (8, length), 1) // LANES
    anchors = [where_ref[0], where_ref[1], where_ref[2]]
    edge_ok = where_ref[3] == 1
    want = jnp.where(line == 0, anchors[0], jnp.where(line == 1, anchors[1], anchors[2]))
    want = jnp.where(line < 3, want, -1)
    qrow_ref[...] = jnp.full(qrow_ref.shape, -2.0, F32)
    krow_ref[...] = jnp.full(krow_ref.shape, -1.0, F32)
    segs, pads = [], []
    for block in range(3):
        start = pl.multiple_of(anchors[block] * LANES, LANES)
        segs.append(row_of(seg_ref[:, pl.ds(start, LANES)], row).astype(F32))
        pads.append(row_of(pad_ref[:, pl.ds(start, LANES)], row))
    for head in range(head_count):
        members = cl_ref[0, head : head + 1, :]
        onehot = (spot == (members % LANES)).astype(F32).astype(BF16)
        chosen = jnp.where((members // LANES) == want, cluster, 0).astype(F32).astype(BF16)
        found = dot_nt(chosen, onehot)
        for block in range(3):
            code = found[block : block + 1, :] * 8.0 + segs[block]
            query, key = code, jnp.where(pads[block] == 1, code, -1.0)
            if block == 2:
                query = jnp.where(edge_ok, query, -2.0)
                key = jnp.where(edge_ok, key, -1.0)
            at = block * 16 + head
            qrow_ref[0, at : at + 1, :] = query
            krow_ref[0, at : at + 1, :] = key
    qrow_ref[0, 48:49, :] = (pads[0] == 1).astype(F32)
    qcol_ref[0] = qrow_ref[0].T
    kcol_ref[0] = krow_ref[0].T


def row_of(block, row):
    chosen = lax.broadcasted_iota(jnp.int32, block.shape, 0) == row
    return jnp.sum(jnp.where(chosen, block, 0), axis=0, keepdims=True)


def cluster_codes(clusters, segment_ids, padding, where_at):
    row_count, head_count, length = clusters.shape
    table = jax.ShapeDtypeStruct((row_count, LANES, LANES), F32)
    spec = pl.BlockSpec((1, LANES, LANES), lambda r, w: (r, 0, 0))
    return pl.pallas_call(
        codes_kernel,
        out_shape=(table,) * 4,
        grid_spec=pltpu.PrefetchScalarGridSpec(
            num_scalar_prefetch=1,
            grid=(row_count,),
            in_specs=[
                pl.BlockSpec((1, head_count, length), lambda r, w: (r, 0, 0)),
                pl.BlockSpec((row_count, length), lambda r, w: (0, 0)),
                pl.BlockSpec((row_count, length), lambda r, w: (0, 0)),
            ],
            out_specs=[spec] * 4,
        ),
        name="codes",
    )(where_at, clusters, segment_ids, padding)


def widen_kernel(*refs):
    for index, ref in enumerate(refs[:-1]):
        refs[-1][index : index + 1, :] = ref[...].astype(F32).reshape(1, ref.shape[0])


def widened(vectors):
    return pl.pallas_call(
        widen_kernel, out_shape=jax.ShapeDtypeStruct((len(vectors),) + vectors[0].shape, F32), name="widen"
    )(*vectors)


def halves(value):
    low = lax.broadcasted_iota(jnp.int32, value.shape, 1) < (LANES // 2)
    zero = jnp.zeros_like(value)
    return jnp.where(low, value, zero), jnp.where(low, zero, value)


def pick(even, odd):
    return jnp.where(lax.broadcasted_iota(jnp.int32, even.shape, 1) < (LANES // 2), even, odd)


def diagonal():
    return lax.broadcasted_iota(jnp.int32, (LANES, LANES), 0) == lax.broadcasted_iota(
        jnp.int32, (LANES, LANES), 1
    )


def attend_kernel(
    model, q_ref, k_ref, v_ref, kc_ref, ke_ref, vc_ref, ve_ref, krow_ref, qcol_ref, ctx_ref, lse_ref, stat_ref
):
    eye = diagonal()
    lane = lax.broadcasted_iota(jnp.int32, (LANES, LANES), 1)
    lse_all = jnp.zeros((LANES, LANES), F32)
    entropy_all = jnp.zeros((LANES, LANES), F32)
    count_all = jnp.ones((LANES, LANES), F32)
    for pair in range(model // LANES):
        at = slice(pair * LANES, (pair + 1) * LANES)
        queries = halves(q_ref[0, :, at])
        keys = jnp.concatenate([r[0, :, at] for r in (k_ref, kc_ref, ke_ref)], axis=0)
        values = jnp.concatenate([r[0, :, at] for r in (v_ref, vc_ref, ve_ref)], axis=0)
        out = []
        for side in range(2):
            head = pair * 2 + side
            raw = dot_nt(queries[side], keys)
            code = qcol_ref[0, :, head : head + 1]
            allowed = [code == krow_ref[0, b * 16 + head : b * 16 + head + 1, :] for b in range(3)]
            allowed[0] = allowed[0] | eye
            allowed = jnp.concatenate(allowed, axis=1)
            masked = jnp.where(allowed, raw, NEGATIVE)
            top = jnp.max(masked, axis=1, keepdims=True)
            grown = jnp.exp(masked - top)
            total = jnp.sum(grown, axis=1, keepdims=True)
            prob = grown * (1.0 / total)
            lse = top + jnp.log(total)
            entropy = lse - jnp.sum(prob * masked, axis=1, keepdims=True)
            count = jnp.sum(jnp.where(allowed, 1.0, 0.0), axis=1, keepdims=True)
            out.append(dot_nn(prob.astype(BF16), values))
            lse_all = jnp.where(lane == head, lse, lse_all)
            entropy_all = jnp.where(lane == head, entropy, entropy_all)
            count_all = jnp.where(lane == head, count, count_all)
        ctx_ref[0, :, at] = pick(out[0], out[1]).astype(BF16)
    real = qcol_ref[0, :, 48:49]
    stat_ref[0] = jnp.zeros(stat_ref.shape[1:], F32)
    stat_ref[0, 0:1, :] = jnp.sum(entropy_all * real, axis=0, keepdims=True)
    stat_ref[0, 1:2, :] = jnp.sum(jnp.log(count_all) * real, axis=0, keepdims=True)
    stat_ref[0, 2:3, :] = jnp.sum(jnp.broadcast_to(real, (LANES, LANES)), axis=0, keepdims=True)
    lse_ref[0] = lse_all.T[:16, :]


def attend(q, k, v, kc, ke, vc, ve, krow, qcol):
    row_count, shard_len, model = q.shape
    own = pl.BlockSpec((1, shard_len, model), lambda r: (r, 0, 0))
    table = pl.BlockSpec((1, LANES, LANES), lambda r: (r, 0, 0))
    return pl.pallas_call(
        lambda *refs: attend_kernel(model, *refs),
        out_shape=(
            jax.ShapeDtypeStruct(q.shape, BF16),
            jax.ShapeDtypeStruct((row_count, 16, LANES), F32),
            jax.ShapeDtypeStruct((row_count, 8, LANES), F32),
        ),
        grid=(row_count,),
        in_specs=[own] * 7 + [table] * 2,
        out_specs=(
            own,
            pl.BlockSpec((1, 16, LANES), lambda r: (r, 0, 0)),
            pl.BlockSpec((1, 8, LANES), lambda r: (r, 0, 0)),
        ),
        name="attend",
    )(q, k, v, kc, ke, vc, ve, krow, qcol)


def pull_query_kernel(
    model, q_ref, k_ref, v_ref, d_ref, kc_ref, ke_ref, vc_ref, ve_ref, row_ref, krow_ref, qcol_ref, out_ref, bias_ref
):
    eye = diagonal()
    cols = jnp.concatenate([row_ref[0], jnp.zeros((LANES - 32, LANES), F32)], axis=0).T
    bias_ref[0] = jnp.zeros(bias_ref.shape[1:], F32)
    for pair in range(model // LANES):
        at = slice(pair * LANES, (pair + 1) * LANES)
        queries, grads = halves(q_ref[0, :, at]), halves(d_ref[0, :, at])
        k_all = jnp.concatenate([r[0, :, at] for r in (k_ref, kc_ref, ke_ref)], axis=0)
        v_all = jnp.concatenate([r[0, :, at] for r in (v_ref, vc_ref, ve_ref)], axis=0)
        dq = []
        for side in range(2):
            head = pair * 2 + side
            code = qcol_ref[0, :, head : head + 1]
            allowed = [code == krow_ref[0, b * 16 + head : b * 16 + head + 1, :] for b in range(3)]
            allowed[0] = allowed[0] | eye
            raw = dot_nt(queries[side], k_all)
            lse, delta = cols[:, head : head + 1], cols[:, 16 + head : 17 + head]
            prob = jnp.exp(jnp.where(jnp.concatenate(allowed, axis=1), raw, NEGATIVE) - lse)
            d_score = (prob * (dot_nt(grads[side], v_all) - delta)).astype(BF16)
            dq.append(dot_nn(d_score, k_all))
        low = pick(dq[0], dq[1]).astype(BF16)
        wide = low.astype(F32) * 0.125
        out_ref[0, :, at] = wide.astype(BF16)
        bias_ref[0, 0:1, at] = jnp.sum(wide, axis=0, keepdims=True)


def pull_pair_kernel(
    model,
    q_ref,
    k_ref,
    v_ref,
    d_ref,
    qc_ref,
    qe_ref,
    dc_ref,
    de_ref,
    row_ref,
    rowc_ref,
    rowe_ref,
    qrow_ref,
    kcol_ref,
    out_ref,
    bias_ref,
):
    eye = diagonal()
    bias_ref[0] = jnp.zeros(bias_ref.shape[1:], F32)
    for pair in range(model // LANES):
        at = slice(pair * LANES, (pair + 1) * LANES)
        keys, values = halves(k_ref[0, :, at]), halves(v_ref[0, :, at])
        q_all = jnp.concatenate([r[0, :, at] for r in (q_ref, qc_ref, qe_ref)], axis=0)
        d_all = jnp.concatenate([r[0, :, at] for r in (d_ref, dc_ref, de_ref)], axis=0)
        dk, dv = [], []
        for side in range(2):
            head = pair * 2 + side
            code = kcol_ref[0, :, head : head + 1]
            allowed = [code == qrow_ref[0, b * 16 + head : b * 16 + head + 1, :] for b in range(3)]
            allowed[0] = allowed[0] | eye
            raw = dot_nt(keys[side], q_all)
            lse = jnp.concatenate([r[0, head : head + 1, :] for r in (row_ref, rowc_ref, rowe_ref)], axis=1)
            delta = jnp.concatenate(
                [r[0, 16 + head : 17 + head, :] for r in (row_ref, rowc_ref, rowe_ref)], axis=1
            )
            prob = jnp.exp(jnp.where(jnp.concatenate(allowed, axis=1), raw, NEGATIVE) - lse)
            d_score = (prob * (dot_nt(values[side], d_all) - delta)).astype(BF16)
            dk.append(dot_nn(d_score, q_all))
            dv.append(dot_nn(prob.astype(BF16), d_all))
        for index, both in enumerate((dk, dv)):
            low = pick(both[0], both[1]).astype(BF16)
            spot = slice(index * model + pair * LANES, index * model + (pair + 1) * LANES)
            out_ref[0, :, spot] = low
            bias_ref[0, 0:1, spot] = jnp.sum(low.astype(F32), axis=0, keepdims=True)


def pull(kernel, copies, activations, lines, tables):
    row_count, shard_len, model = activations[0].shape
    own = pl.BlockSpec((1, shard_len, model), lambda r: (r, 0, 0))
    table = pl.BlockSpec((1, LANES, LANES), lambda r: (r, 0, 0))
    line = pl.BlockSpec((1, 32, LANES), lambda r: (r, 0, 0))
    return pl.pallas_call(
        lambda *refs: kernel(model, *refs),
        out_shape=(
            jax.ShapeDtypeStruct((row_count, shard_len, copies * model), BF16),
            jax.ShapeDtypeStruct((row_count, 8, copies * model), F32),
        ),
        grid=(row_count,),
        in_specs=[own] * len(activations) + [line] * len(lines) + [table] * len(tables),
        out_specs=(
            pl.BlockSpec((1, shard_len, copies * model), lambda r: (r, 0, 0)),
            pl.BlockSpec((1, 8, copies * model), lambda r: (r, 0, 0)),
        ),
    )(*activations, *lines, *tables)


def normed(value):
    centred = value - jnp.mean(value, axis=-1, keepdims=True)
    inverse = lax.rsqrt(jnp.mean(centred * centred, axis=-1, keepdims=True) + EPSILON)
    return centred * inverse, inverse


def norm_pull(grad, gain, unit, inverse):
    scaled = grad * gain
    moved = scaled - jnp.mean(scaled, axis=-1, keepdims=True)
    moved = moved - unit * jnp.mean(scaled * unit, axis=-1, keepdims=True)
    return moved * inverse


def gelu_both(value):
    cdf = 0.5 * (1.0 + lax.erf(value * (0.5**0.5)))
    return value * cdf, cdf + value * (jnp.exp(-0.5 * value * value) * 0.3989422804014327)


class Links:
    def __init__(self, dp_size, seq_size):
        self.dp, self.seq = dp_size, seq_size
        self.dp_at, self.seq_at = lax.axis_index("dp"), lax.axis_index("seq")
        self.bits = [1 << n for n in range(1, dp_size.bit_length() - 1)]

    def swap(self, value, dp_bits, seq_bits):
        pairs = [
            (d * self.seq + s, (d ^ dp_bits) * self.seq + (s ^ seq_bits))
            for d in range(self.dp)
            for s in range(self.seq)
        ]
        return lax.ppermute(value, AXES, pairs)

    def edge(self, value):
        pairs = []
        for d in range(self.dp):
            for s in range(1, self.seq - 1, 2):
                pairs.append((d * self.seq + s, d * self.seq + s + 1))
                pairs.append((d * self.seq + s + 1, d * self.seq + s))
        return lax.ppermute(value, AXES, pairs)

    def dp_stage(self, bit):
        return [(0, 0), (bit, 0)], (self.dp_at // bit) % 2, "x" if bit == 1 else "z%d" % bit

    def y_stage(self):
        return [(0, 0), (0, 2)], self.seq_at // 2, "y"

    def plane(self):
        return [(j & 1, (j >> 1) * 2) for j in range(4)], (self.dp_at % 2) + 2 * (self.seq_at // 2), "p"

    def z_stages(self):
        return [self.dp_stage(bit) for bit in self.bits]

    def spread(self, value, stage, axis=0):
        partners, mine, _ = stage
        rows = value.shape[axis] // len(partners)
        total = lax.dynamic_slice_in_dim(value, mine * rows, rows, axis).astype(F32)
        for index in range(1, len(partners)):
            sent = lax.dynamic_slice_in_dim(value, (mine ^ index) * rows, rows, axis)
            total = total + self.swap(sent, *partners[index]).astype(F32)
        return total.astype(BF16)

    def collect(self, value, stage, axis=0):
        partners, mine, _ = stage
        pieces = [value]
        for index in range(1, len(partners)):
            pieces.append(self.swap(value, *partners[index]))
        bit = 1
        while bit < len(pieces):
            odd = (mine // bit) % 2 == 1
            pieces = [jnp.where(odd, pieces[n ^ bit], pieces[n]) for n in range(len(pieces))]
            bit *= 2
        return jnp.concatenate(pieces, axis=axis)

    def core_spread(self, value):
        mine = self.seq_at % 2
        cols = value.shape[1] // 2
        keep = lax.dynamic_slice_in_dim(value, mine * cols, cols, 1)
        sent = lax.dynamic_slice_in_dim(value, (1 - mine) * cols, cols, 1)
        return (keep.astype(F32) + self.swap(sent, 0, 1).astype(F32)).astype(BF16)

    def core_collect(self, value):
        mine = self.seq_at % 2
        other = self.swap(value, 0, 1)
        return jnp.where(mine == 0, value, other), jnp.where(mine == 0, other, value)

    def carried(self, value, small):
        mine = self.seq_at % 2
        cols = value.shape[1] // 2
        keep = lax.dynamic_slice_in_dim(value, mine * cols, cols, 1)
        sent = lax.dynamic_slice_in_dim(value, (1 - mine) * cols, cols, 1)
        got = self.swap(jnp.concatenate([sent, small], axis=0), 0, 1).astype(F32)
        value = (keep.astype(F32) + got[: value.shape[0]]).astype(BF16)
        small = (small.astype(F32) + got[value.shape[0] :]).astype(BF16)
        partners, mine, _ = self.plane()
        rows = value.shape[0] // len(partners)
        got = [None] * len(partners)
        for index in range(1, len(partners)):
            sent = lax.dynamic_slice_in_dim(value, (mine ^ index) * rows, rows, 0)
            sent = jnp.concatenate([sent, small], axis=0)
            got[index] = self.swap(sent, *partners[index]).astype(F32)
        own = lax.dynamic_slice_in_dim(value, mine * rows, rows, 0)
        own = jnp.concatenate([own, small], axis=0).astype(F32)
        value = (own + got[1]) + (got[2] + got[3])
        for bit in self.bits:
            value = value.astype(BF16)
            value = value.astype(F32) + self.swap(value, bit, 0).astype(F32)
        return value[:rows].astype(BF16), value[rows:]

    def doubled(self, value):
        for bit in self.bits:
            other = self.swap(value, bit, 0)
            value = (value.astype(F32) + other.astype(F32)).astype(BF16)
        return value

    def around(self, value, stages, axis=0):
        for stage in stages:
            value = self.spread(value, stage, axis)
        for stage in reversed(stages):
            value = self.collect(value, stage, axis)
        return value


def body(
    tokens,
    segment_ids,
    padding,
    clusters,
    w_query,
    w_key,
    w_value,
    w_output,
    b_query,
    b_value,
    b_output,
    gain_attn,
    shift_attn,
    w_inner,
    b_inner,
    w_outer,
    b_outer,
    gain_ffn,
    shift_ffn,
    cotangent,
):
    links = Links(lax.axis_size("dp"), lax.axis_size("seq"))
    seq_at, seq_count = links.seq_at, links.seq
    row_count, shard_len, model = tokens.shape
    head_count = clusters.shape[1]
    amount = row_count * shard_len
    own_shape = (row_count, shard_len, model)
    tokens_edge = links.edge(tokens)
    tokens_core = links.swap(tokens, 0, 1)
    inner, outer, inner_bias = [w_inner], [w_outer], [b_inner[None, :]]
    inner.append(links.swap(w_inner, 0, 2))
    outer.append(links.swap(w_outer, 0, 2))
    inner_bias.append(links.swap(inner_bias[0], 0, 2))
    for index in range(2):
        inner.append(links.swap(inner[index], 0, 1))
        outer.append(links.swap(outer[index], 0, 1))
    both = links.swap(jnp.concatenate(inner_bias, axis=0), 0, 1)
    inner_bias += [both[0:1], both[1:2]]

    line = lax.broadcasted_iota(jnp.int32, (4,), 0)
    edge_raw = jnp.where(seq_at % 2 == 1, seq_at + 1, seq_at - 1)
    edge_ok = (edge_raw >= 0) & (edge_raw < seq_count)
    where_at = jnp.where(line == 2, jnp.clip(edge_raw, 0, seq_count - 1), edge_ok.astype(jnp.int32))
    where_at = jnp.where(line == 0, seq_at, jnp.where(line == 1, seq_at ^ 1, where_at)).astype(jnp.int32)
    qrow, krow, qcol, kcol = cluster_codes(clusters, segment_ids, padding, where_at)
    vectors = [b_query, b_value, b_output, gain_attn, shift_attn, b_outer, gain_ffn, shift_ffn]
    vectors = widened(vectors)
    bias_query, bias_value, bias_output, gain_one, shift_one, bias_outer, gain_two, shift_two = [
        vectors[n : n + 1] for n in range(8)
    ]

    def make_query(array):
        return ((dot_nn(array, w_query) + bias_query) * 0.125).astype(BF16).reshape(own_shape)

    def make_key(array):
        return dot_nn(array, w_key).astype(BF16).reshape(own_shape)

    def make_value(array):
        return (dot_nn(array, w_value) + bias_value).astype(BF16).reshape(own_shape)

    flat = tokens.reshape(amount, model)
    flat_core, flat_edge = tokens_core.reshape(amount, model), tokens_edge.reshape(amount, model)
    q, k, v = make_query(flat), make_key(flat), make_value(flat)
    k_core, v_core = make_key(flat_core), make_value(flat_core)
    k_edge, v_edge = make_key(flat_edge), make_value(flat_edge)
    context, lse, stats = attend(q, k, v, k_core, k_edge, v_core, v_edge, krow, qcol)
    q_core, q_edge = make_query(flat_core), make_query(flat_edge)
    context = context.reshape(amount, model)

    x = flat.astype(F32)
    residual_one = x + dot_nn(context, w_output) + bias_output
    unit_one, inverse_one = normed(residual_one)
    mid = unit_one * gain_one + shift_one
    mid_low = mid.astype(BF16)

    acts, slopes = [None] * 4, [None] * 4
    residual_two = mid + bias_outer
    for index in (0, 2, 1, 3):
        act, slopes[index] = gelu_both(dot_nn(mid_low, inner[index]) + inner_bias[index].astype(F32))
        acts[index] = act.astype(BF16)
        residual_two = residual_two + dot_nn(acts[index], outer[index])
    unit_two, inverse_two = normed(residual_two)
    output = (unit_two * gain_two + shift_two).astype(BF16)
    grad = cotangent.reshape(amount, model).astype(F32)
    d_two = norm_pull(grad, gain_two, unit_two, inverse_two)
    d_two_low = d_two.astype(BF16)

    grads_inner, grads_outer = [None] * 4, [None] * 4

    def far_of(parts):
        return parts[1] + links.swap(parts[3].astype(BF16), 0, 1).astype(F32)

    def near_of(parts):
        return parts[0] + links.swap(parts[2].astype(BF16), 0, 1).astype(F32)

    for index in (3, 1, 2, 0):
        grads_outer[index] = dot_tn(acts[index], d_two_low)
    far = far_of(grads_outer).astype(BF16)
    near = near_of(grads_outer)
    grad_outer = (near + links.swap(far, 0, 2).astype(F32)).astype(BF16)

    d_mid = d_two
    grads_bias = [None] * 4
    for index in (0, 2, 1, 3):
        d_pre = (slopes[index] * dot_nt(d_two_low, outer[index])).astype(BF16)
        grads_bias[index] = jnp.sum(d_pre.astype(F32), axis=0, keepdims=True)
        d_mid = d_mid + dot_nt(d_pre, inner[index])
        grads_inner[index] = dot_tn(mid_low, d_pre)

    d_one = norm_pull(d_mid, gain_one, unit_one, inverse_one)
    d_one_low = d_one.astype(BF16)
    d_context = dot_nt(d_one_low, w_output).astype(BF16)
    d_context_own = d_context.reshape(own_shape)
    d_edge = links.edge(d_context_own)
    d_core = links.swap(d_context_own, 0, 1)
    head_of = lax.broadcasted_iota(jnp.int32, (16, model), 1) // (model // head_count)
    head_sum = (head_of == lax.broadcasted_iota(jnp.int32, (16, model), 0)).astype(F32)
    delta = lax.dot_general(
        head_sum,
        d_context.astype(F32) * context.astype(F32),
        (((1,), (1,)), ((), ())),
        precision=lax.Precision.HIGHEST,
        preferred_element_type=F32,
    )
    delta = jnp.transpose(delta.reshape(16, row_count, shard_len), (1, 0, 2))
    lines = jnp.concatenate([lse, delta], axis=1)
    lines_edge = links.edge(lines)
    lines_core = links.swap(lines, 0, 1)

    pair = jnp.stack([near_of(grads_inner), far_of(grads_inner)]).astype(BF16)
    pair = links.spread(pair, links.dp_stage(1), 1)
    grad_inner = pair[0].astype(F32) + links.swap(pair[1], 0, 2).astype(F32)
    grad_inner = links.around(grad_inner.astype(BF16), links.z_stages())
    grad_inner = links.collect(grad_inner, links.dp_stage(1)).astype(F32)

    grad_outer = links.spread(grad_outer, links.dp_stage(1))
    grad_outer = links.around(grad_outer, links.z_stages())
    grad_outer = links.collect(grad_outer, links.dp_stage(1))
    grad_outer = grad_outer.astype(F32)

    d_query, bias_dq = pull(
        pull_query_kernel, 1, [q, k, v, d_context_own, k_core, k_edge, v_core, v_edge], [lines], [krow, qcol]
    )
    d_query = d_query.reshape(amount, model)
    grad_w_output = dot_tn(context, d_one_low).astype(BF16)
    grad_w_query = dot_tn(flat, d_query).astype(BF16)
    first = jnp.stack([links.core_spread(grad_w_output), links.core_spread(grad_w_query)])
    for stage in (links.y_stage(), links.dp_stage(1)):
        first = links.spread(first, stage, 1)
    first = links.doubled(first)
    for stage in (links.dp_stage(1), links.y_stage()):
        first = links.collect(first, stage, 1)
    low, high = links.core_collect(first)
    grad_w_output, grad_w_query = [jnp.concatenate([low[n], high[n]], axis=1).astype(F32) for n in range(2)]

    d_pair, bias_pair = pull(
        pull_pair_kernel,
        2,
        [q, k, v, d_context_own, q_core, q_edge, d_core, d_edge],
        [lines, lines_core, lines_edge],
        [qrow, kcol],
    )
    d_pair = d_pair.reshape(amount, 2 * model)
    last = dot_tn(flat, d_pair).astype(BF16)
    grad_tokens = (
        d_one
        + dot_nt(d_query, w_query)
        + dot_nt(d_pair[:, :model], w_key)
        + dot_nt(d_pair[:, model:], w_value)
    ).astype(BF16)

    bias_rows = [grads_bias[n] for n in (0, 2, 1, 3)]
    for bit in (1, 2):
        odd = (seq_at // bit) % 2 == 1
        bias_rows = [jnp.where(odd, bias_rows[n ^ bit], bias_rows[n]) for n in range(4)]
    stat_rows = jnp.sum(stats, axis=0)[0:3, :]
    stat_rows = jnp.pad(stat_rows, ((0, 0), (0, model - LANES)))
    small = [jnp.sum(bias_dq[:, 0:1, :], axis=0), jnp.sum(bias_pair[:, 0:1, model:], axis=0)]
    small += [jnp.sum(value, axis=0, keepdims=True) for value in (d_one, d_mid * unit_one, d_mid, d_two, grad * unit_two, grad)]
    small += [stat_rows] + bias_rows
    small = jnp.concatenate(small, axis=0)
    small = jnp.pad(small, ((0, -small.shape[0] % 16), (0, 0))).astype(BF16)
    last, small = links.carried(last, small)
    last = links.collect(last, links.plane())
    grad_w_key, grad_w_value = [half.astype(F32) for half in links.core_collect(last)]
    cluster_log = small[8:10, :head_count] / small[10:11, 0:1]
    return (
        output.reshape(own_shape),
        grad_tokens.reshape(own_shape),
        grad_w_query,
        grad_w_key,
        grad_w_value,
        grad_w_output,
        small[0],
        small[1],
        small[2],
        small[3],
        small[4],
        grad_inner,
        lax.dynamic_index_in_dim(small[11:15], seq_at, 0, False),
        grad_outer,
        small[5],
        small[6],
        small[7],
        cluster_log,
    )


def solution(mesh):
    return jax.shard_map(
        body,
        mesh=mesh,
        in_specs=(
            P("dp", "seq", None),
            P("dp", None),
            P("dp", None),
            P("dp", None, None),
            P(),
            P(),
            P(),
            P(),
            P(),
            P(),
            P(),
            P(),
            P(),
            P(None, "seq"),
            P("seq"),
            P("seq", None),
            P(),
            P(),
            P(),
            P("dp", "seq", None),
        ),
        out_specs=(
            P("dp", "seq", None),
            P("dp", "seq", None),
            P(),
            P(),
            P(),
            P(),
            P(),
            P(),
            P(),
            P(),
            P(),
            P(None, "seq"),
            P("seq"),
            P("seq", None),
            P(),
            P(),
            P(),
            P(),
        ),
        check_vma=False,
    )
```
